128 devices in a mesh: queue: 4 (over y), dp: 32 (over x, z, core).
Axes of the slice: x: 4, y: 4, z: 4, core: 2. Of those that a mesh axis runs over, the one named last changes fastest.
Arguments:
- features: bfloat16 [4096, 49, 2048], P(('queue', 'dp')), may hold values from -40 to 40
- shuffle: int32 [4, 1024], P('queue'), may hold values from 0 to 1023, as said below
- positive: int32 [4096], P(('queue', 'dp')), may hold values from 0 to 1023, as said below
- queries: bfloat16 [4096, 128], P(('queue', 'dp')), may hold values from -8 to 8
- queue_keys: bfloat16 [65536, 128], P('queue'), may hold values from -8 to 8
- reduce_weight: bfloat16 [2048, 512], replicated, may hold values from -0.125 to 0.125
- gain_one: float32 [512], replicated, may hold values from 0.1 to 1.9
- shift_one: float32 [512], replicated, may hold values from -3 to 3
- w_spatial: bfloat16 [9, 512, 512], replicated, may hold values from -0.09375 to 0.09375
- gain_two: float32 [512], replicated, may hold values from 0.1 to 1.9
- shift_two: float32 [512], replicated, may hold values from -3 to 3
- w_expand: bfloat16 [512, 2048], replicated, may hold values from -0.25 to 0.25
- gain_three: float32 [2048], replicated, may hold values from 0.1 to 1.9
- shift_three: float32 [2048], replicated, may hold values from -3 to 3
- w_project: bfloat16 [2048, 128], replicated, may hold values from -0.125 to 0.125
Outputs:
- loss_vals: float32 [4096], P(('queue', 'dp'))
- key_rows: bfloat16 [4096, 128], P(('queue', 'dp'))
The draws below stay inside these ranges and needn't reach their ends.
Inputs may be any that keep to these rules, and one draw needn't show every extreme that they name: `shuffle`: each row is a permutation of 0 to 1023, and each block of 32 slots k * 32 to (k + 1) * 32 - 1 holds exactly one image from each block of 32 images. Within each queue group of 1024 queries, positive is a permutation of 0 to 1023.
All inputs are finite; a program needn't handle non-finite values.
Results may differ from the reference program's by a relative error of at most 0.0075.
Values may be sent and summed in bfloat16 or wider, within the bound.
No kernel may reach another device: no remote copies, remote signals or barrier semaphores. Data moves between devices by JAX's collectives and lax.ppermute only.
A program may use at most 128 MiB of HBM per device.

```python
import math
import jax
import jax.numpy as jnp
from jax import lax

C = 2048
MID = 512
SIDE = 7
FEAT = 128
QUEUE_LEN = 65536
IMG_DEV = 32
GROUP = 1024
GROUPS = 4
BATCH = 4096


def shared_basis(key):
    basis = jax.random.normal(jax.random.fold_in(key, 4711), (4, FEAT), jnp.float32)
    return basis / jnp.sqrt(jnp.sum(basis * basis, 1, keepdims=True))


def draw_features(key, part):
    subkeys = jax.random.split(key, 4)
    channel_scale = jnp.exp(jax.random.uniform(subkeys[0], (1, 1, C), jnp.float32, math.log(0.3), math.log(3.0)))
    offset = jnp.clip(jax.random.normal(subkeys[1], (BATCH, 1, C), jnp.float32), -4.0, 4.0) * 0.8 * channel_scale
    image_scale = jnp.exp(jax.random.uniform(subkeys[2], (BATCH, 1, 1), jnp.float32, math.log(0.3), math.log(3.0)))
    jitter = jnp.clip(jax.random.normal(subkeys[3], (BATCH, SIDE * SIDE, C), jnp.float32), -4.0, 4.0)
    return jnp.clip(image_scale * (offset + jitter), -40.0, 40.0).astype(jnp.bfloat16)


def one_shuffle(subkey):
    dev_count = GROUP // IMG_DEV
    per_peer = IMG_DEV // dev_count
    first_key, second_key = jax.random.split(subkey)
    local_sets = jax.vmap(lambda inner: jax.random.permutation(inner, IMG_DEV))(jax.random.split(first_key, dev_count))
    local_sets = local_sets + (jnp.arange(dev_count, dtype=jnp.int32) * IMG_DEV)[:, None]
    arranged = local_sets.reshape(dev_count, dev_count, per_peer).transpose(1, 0, 2).reshape(dev_count, IMG_DEV)
    arrival_order = jax.vmap(lambda inner: jax.random.permutation(inner, IMG_DEV))(jax.random.split(second_key, dev_count))
    return jnp.take_along_axis(arranged, arrival_order, 1).reshape(GROUP).astype(jnp.int32)


def draw_shuffle(key, part):
    return jax.vmap(one_shuffle)(jax.random.split(key, GROUPS)).astype(jnp.int32)


def draw_positive(key, part):
    rows = jax.vmap(lambda inner: jax.random.permutation(inner, GROUP))(jax.random.split(jax.random.fold_in(key, 99), GROUPS))
    return rows.reshape(BATCH).astype(jnp.int32)


def draw_queries(key, part):
    basis = shared_basis(key)
    subkeys = jax.random.split(jax.random.fold_in(key, 11), 2)
    jitter = jax.random.normal(subkeys[1], (BATCH, FEAT), jnp.float32) / math.sqrt(FEAT)
    coeff = jnp.clip(jax.random.normal(subkeys[0], (BATCH, 3), jnp.float32), -3.0, 3.0)
    values = jnp.dot(coeff, basis[:3]) + basis[3][None, :] + 0.3 * jitter
    return jnp.clip(values / 4.0, -8.0, 8.0).astype(jnp.bfloat16)


def draw_queue_keys(key, part):
    basis = shared_basis(key)
    subkeys = jax.random.split(jax.random.fold_in(key, 23), 2)
    coeff = jnp.clip(jax.random.normal(subkeys[0], (QUEUE_LEN, 3), jnp.float32), -3.0, 3.0)
    jitter = jax.random.normal(subkeys[1], (QUEUE_LEN, FEAT), jnp.float32) / math.sqrt(FEAT)
    ramp_level = 1.5 * jnp.arange(QUEUE_LEN, dtype=jnp.float32) / QUEUE_LEN
    values = jnp.dot(coeff, basis[:3]) + ramp_level[:, None] * basis[3][None, :] + 0.3 * jitter
    return jnp.clip(values, -8.0, 8.0).astype(jnp.bfloat16)


def scatter_about(key, dims, deviation, bound, kind=jnp.bfloat16):
    result = deviation * jax.random.normal(key, dims, jnp.float32)
    return jnp.clip(result, min=-bound, max=bound).astype(kind)


def setup_inputs(seed: int = 0) -> dict:
    key_of = jax.random.split(jax.random.key(seed), 16)
    features = draw_features(jax.random.fold_in(key_of[15], 71), 0)
    shuffle = draw_shuffle(jax.random.fold_in(key_of[15], 71), 0)
    positive = draw_positive(jax.random.fold_in(key_of[15], 71), 0)
    queries = draw_queries(jax.random.fold_in(key_of[15], 71), 0)
    queue_keys = draw_queue_keys(jax.random.fold_in(key_of[15], 71), 0)
    reduce_weight = scatter_about(key_of[5], (C, MID), C ** -0.5, 0.125)
    gain_one = jnp.clip(1.0 + 0.18 * jax.random.normal(key_of[6], (MID,), jnp.float32), 0.1, 1.9)
    shift_one = scatter_about(key_of[7], (MID,), 0.5, 3.0, jnp.float32)
    w_spatial = scatter_about(key_of[8], (9, MID, MID), (9 * MID) ** -0.5, 0.09375)
    gain_two = jnp.clip(1.0 + 0.18 * jax.random.normal(key_of[9], (MID,), jnp.float32), 0.1, 1.9)
    shift_two = scatter_about(key_of[10], (MID,), 0.5, 3.0, jnp.float32)
    w_expand = scatter_about(key_of[11], (MID, C), MID ** -0.5, 0.25)
    gain_three = jnp.clip(1.0 + 0.18 * jax.random.normal(key_of[12], (C,), jnp.float32), 0.1, 1.9)
    shift_three = scatter_about(key_of[13], (C,), 0.5, 3.0, jnp.float32)
    w_project = scatter_about(key_of[14], (C, FEAT), C ** -0.5, 0.125)
    return dict(features=features, shuffle=shuffle, positive=positive, queries=queries, queue_keys=queue_keys, reduce_weight=reduce_weight, gain_one=gain_one, shift_one=shift_one, w_spatial=w_spatial, gain_two=gain_two, shift_two=shift_two, w_expand=w_expand, gain_three=gain_three, shift_three=shift_three, w_project=w_project)


norm_epsilon = 1e-05
unit_epsilon = 1e-06
sharpness_divisor = 0.2

def moments(first_sums, second_sums, row_count):
    average = first_sums / row_count
    spread = second_sums / row_count - average * average
    return (average, lax.rsqrt(spread + norm_epsilon))

def normalized(values, average, inv_scale, gain_vec, shift_vector):
    return (values - average) * inv_scale * gain_vec + shift_vector

def whole_set(values):
    row_count = values.shape[0] * values.shape[1]
    average, inv_scale = moments(lax.optimization_barrier(jnp.sum(values, (0, 1))), lax.optimization_barrier(jnp.sum(values * values, (0, 1))), row_count)
    return (average[None, None, :], inv_scale[None, None, :])

def unit_rows(values):
    as_float = values.astype(jnp.float32)
    return (as_float * lax.rsqrt(lax.optimization_barrier(jnp.sum(as_float * as_float, -1, keepdims=True)) + unit_epsilon)).astype(jnp.bfloat16)

def conv_three(first_act, w_spatial):
    image_count, location_indices, inner_width = first_act.shape
    grid = first_act.reshape(image_count, SIDE, SIDE, inner_width)
    padded = jnp.pad(grid, ((0, 0), (1, 1), (1, 1), (0, 0)))
    summed = jnp.zeros((image_count * location_indices, w_spatial.shape[2]), jnp.float32)
    for offset in range(9):
        row_shift = offset // 3
        col_shift = offset % 3
        window = padded[:, row_shift:row_shift + SIDE, col_shift:col_shift + SIDE, :].reshape(-1, inner_width)
        summed = summed + jnp.dot(window, w_spatial[offset], preferred_element_type=jnp.float32)
    return summed.reshape(image_count, location_indices, -1)

def encode_tail(first_out, residual, set_moments, gain_one, shift_one, w_spatial, gain_two, shift_two, w_expand, gain_three, shift_three, w_project):
    average, inv_scale = set_moments(first_out)
    first_act = jnp.maximum(normalized(first_out, average, inv_scale, gain_one, shift_one), 0.0).astype(jnp.bfloat16)
    spatial = conv_three(first_act, w_spatial)
    average, inv_scale = set_moments(spatial)
    second_act = jnp.maximum(normalized(spatial, average, inv_scale, gain_two, shift_two), 0.0).astype(jnp.bfloat16)
    image_count, location_indices, inner_width = second_act.shape
    expanded = jnp.dot(second_act.reshape(-1, inner_width), w_expand, preferred_element_type=jnp.float32)
    expanded = expanded.reshape(image_count, location_indices, -1)
    average, inv_scale = set_moments(expanded)
    merged = jnp.maximum(normalized(expanded, average, inv_scale, gain_three, shift_three) + residual.astype(jnp.float32), 0.0)
    pooled = lax.optimization_barrier(jnp.mean(merged, 1)).astype(jnp.bfloat16)
    return unit_rows(jnp.dot(pooled, w_project, preferred_element_type=jnp.float32))

def reference(features, shuffle, positive, queries, queue_keys, reduce_weight, gain_one, shift_one, w_spatial, gain_two, shift_two, w_expand, gain_three, shift_three, w_project):
    channels = features.shape[2]
    location_indices = features.shape[1]
    set_ids = (shuffle + (jnp.arange(GROUPS, dtype=jnp.int32) * GROUP)[:, None]).reshape(-1, IMG_DEV).astype(jnp.int32)

    def one_set(image_ids):
        images = features[image_ids]
        first_out = jnp.dot(images.reshape(-1, channels), reduce_weight, preferred_element_type=jnp.float32)
        first_out = first_out.reshape(IMG_DEV, location_indices, -1)
        return encode_tail(first_out, images, whole_set, gain_one, shift_one, w_spatial, gain_two, shift_two, w_expand, gain_three, shift_three, w_project)
    keyed = lax.map(one_set, set_ids)
    key_rows = jnp.zeros((BATCH, FEAT), jnp.bfloat16).at[set_ids.reshape(-1)].set(keyed.reshape(-1, FEAT))
    unitlength_probe = unit_rows(queries)
    slice_base = (jnp.arange(BATCH, dtype=jnp.int32) // GROUP * GROUP).astype(jnp.int32)
    paired_encodings = key_rows[slice_base + positive]
    paired_affinity = lax.optimization_barrier(jnp.sum(unitlength_probe.astype(jnp.float32) * paired_encodings.astype(jnp.float32), 1)) / sharpness_divisor
    unit_queue = unit_rows(queue_keys)

    def negative_scores_for(query_block):
        affinity_matrix = lax.dot_general(query_block, unit_queue, (((1,), (1,)), ((), ())), preferred_element_type=jnp.float32)
        return lax.optimization_barrier(jnp.sum(jnp.exp(affinity_matrix / sharpness_divisor), 1))
    negatives = lax.map(negative_scores_for, unitlength_probe.reshape(-1, 512, FEAT)).reshape(BATCH)
    loss_vals = jnp.log(jnp.exp(paired_affinity) + negatives) - paired_affinity
    return (loss_vals, key_rows)
```

```python
import functools
import math

import jax
import jax.numpy as jnp
from jax import lax
from jax.experimental import pallas as pl
from jax.experimental.pallas import tpu as pltpu
from jax.sharding import PartitionSpec as P

SIDE = 7
EPS = 1e-05
UNIT_EPS = 1e-06
TEMP = 0.2
HIGH = lax.Precision.HIGHEST
F32 = jnp.float32
BF16 = jnp.bfloat16
VMEM = pl.BlockSpec(memory_space=pltpu.VMEM)
SMEM = pl.BlockSpec(memory_space=pltpu.SMEM)


def params(limit_mib):
    return pltpu.CompilerParams(
        dimension_semantics=("arbitrary",), vmem_limit_bytes=limit_mib * 1024 * 1024
    )


def dot32(a, b):
    return jnp.dot(a, b, preferred_element_type=F32)


def pick_rows(onehot, values):
    return lax.dot_general(
        onehot, values, (((1,), (0,)), ((), ())), precision=HIGH, preferred_element_type=F32
    )


def unpick_rows(onehot, values):
    return lax.dot_general(
        onehot, values, (((0,), (0,)), ((), ())), precision=HIGH, preferred_element_type=F32
    )


def split_halves(core, values, keep_ref, send_ref, start):
    half = values.shape[1] // 2
    low, high = values[:, :half], values[:, half:]
    keep_ref[:, start : start + half] = jnp.where(core == 0, low, high)
    send_ref[:, start : start + half] = jnp.where(core == 0, high, low)


def join_halves(core, mine, other):
    low = jnp.where(core == 0, mine, other)
    high = jnp.where(core == 0, other, mine)
    return jnp.concatenate([low, high], 1)


def reduce_kernel(core_ref, x_ref, w_ref, p_ref, y_ref, keep_ref, send_ref, s1, s2):
    step = pl.program_id(0)

    @pl.when(step == 0)
    def _():
        s1[...] = jnp.zeros_like(s1)
        s2[...] = jnp.zeros_like(s2)

    side, count, channels = x_ref.shape
    y = dot32(x_ref[...].reshape(side * count, channels), w_ref[...])
    y = y.reshape(side, count, -1)
    y_ref[...] = y
    s1[...] += jnp.sum(y, 0)
    s2[...] += jnp.sum(y * y, 0)

    @pl.when(step == pl.num_programs(0) - 1)
    def _():
        core = core_ref[0]
        onehot = p_ref[...]
        split_halves(core, pick_rows(onehot, s1[...]), keep_ref, send_ref, 0)
        half = s1.shape[1] // 2
        split_halves(core, pick_rows(onehot, s2[...]), keep_ref, send_ref, half)


def reduce_stage(core, x, weight, onehot):
    places, count, channels = x.shape
    mid = weight.shape[1]
    return pl.pallas_call(
        reduce_kernel,
        name="reduce",
        grid=(places // SIDE,),
        in_specs=[
            SMEM,
            pl.BlockSpec((SIDE, count, channels), lambda i: (i, 0, 0)),
            VMEM,
            VMEM,
        ],
        out_specs=[
            pl.BlockSpec((SIDE, count, mid), lambda i: (i, 0, 0)),
            pl.BlockSpec((count, mid), lambda i: (0, 0)),
            pl.BlockSpec((count, mid), lambda i: (0, 0)),
        ],
        out_shape=[
            jax.ShapeDtypeStruct((places, count, mid), F32),
            jax.ShapeDtypeStruct((count, mid), F32),
            jax.ShapeDtypeStruct((count, mid), F32),
        ],
        scratch_shapes=[pltpu.VMEM((count, mid), F32), pltpu.VMEM((count, mid), F32)],
        compiler_params=params(12),
        cost_estimate=pl.CostEstimate(
            flops=2 * places * count * channels * mid,
            bytes_accessed=2 * x.size + 4 * places * count * mid,
            transcendentals=0,
        ),
    )(core, x, weight, onehot)


def scale_shift(core, mine, other, onehot, gain, shift, rows):
    half = mine.shape[1] // 2
    total1 = join_halves(core, mine[:, :half], other[:, :half])
    total2 = join_halves(core, mine[:, half:], other[:, half:])
    average = total1 / rows
    spread = total2 / rows - average * average
    scale = lax.rsqrt(spread + EPS) * gain
    return unpick_rows(onehot, scale), unpick_rows(onehot, shift - average * scale)


def conv_kernel(
    rows,
    core_ref,
    y_ref,
    mine_ref,
    other_ref,
    p_ref,
    gain_ref,
    shift_ref,
    w_ref,
    z_ref,
    keep_ref,
    send_ref,
    act,
    scale_s,
    shift_s,
    s1,
    s2,
):
    step = pl.program_id(0)
    side, count, mid = y_ref.shape

    @pl.when(step == 0)
    def _():
        scale, shift = scale_shift(
            core_ref[0], mine_ref[...], other_ref[...], p_ref[...], gain_ref[...], shift_ref[...], rows
        )
        scale_s[...] = scale
        shift_s[...] = shift
        s1[...] = jnp.zeros_like(s1)
        s2[...] = jnp.zeros_like(s2)

    @pl.when(step < side)
    def _():
        a = jnp.maximum(y_ref[...] * scale_s[...][None] + shift_s[...][None], 0.0)
        act[step] = a.astype(BF16)

    out = step - 1

    def taps(row, dy, first):
        for dx in (0, -1, 1):
            lo, hi = max(0, -dx), side - max(0, dx)
            window = act[row, lo + dx : hi + dx].reshape((hi - lo) * count, mid)
            part = dot32(window, w_ref[3 * (dy + 1) + dx + 1]).reshape(hi - lo, count, mid)
            if first and dx == 0:
                z_ref[...] = part
            else:
                z_ref[lo:hi] += part

    @pl.when(step >= 1)
    def _():
        taps(out, 0, True)

        @pl.when(out >= 1)
        def _():
            taps(out - 1, -1, False)

        @pl.when(out + 1 < side)
        def _():
            taps(out + 1, 1, False)

        z = z_ref[...]
        s1[...] += jnp.sum(z, 0)
        s2[...] += jnp.sum(z * z, 0)

    @pl.when(step == side)
    def _():
        core = core_ref[0]
        onehot = p_ref[...]
        split_halves(core, pick_rows(onehot, s1[...]), keep_ref, send_ref, 0)
        split_halves(core, pick_rows(onehot, s2[...]), keep_ref, send_ref, mid // 2)


def conv_stage(rows, core, y, mine, other, onehot, gain, shift, weight):
    places, count, mid = y.shape
    return pl.pallas_call(
        functools.partial(conv_kernel, rows),
        name="conv",
        grid=(SIDE + 1,),
        in_specs=[
            SMEM,
            pl.BlockSpec((SIDE, count, mid), lambda i: (jnp.minimum(i, SIDE - 1), 0, 0)),
            VMEM,
            VMEM,
            VMEM,
            VMEM,
            VMEM,
            VMEM,
        ],
        out_specs=[
            pl.BlockSpec((SIDE, count, mid), lambda i: (jnp.maximum(i - 1, 0), 0, 0)),
            pl.BlockSpec((count, mid), lambda i: (0, 0)),
            pl.BlockSpec((count, mid), lambda i: (0, 0)),
        ],
        out_shape=[
            jax.ShapeDtypeStruct((places, count, mid), F32),
            jax.ShapeDtypeStruct((count, mid), F32),
            jax.ShapeDtypeStruct((count, mid), F32),
        ],
        scratch_shapes=[
            pltpu.VMEM((SIDE, SIDE, count, mid), BF16),
            pltpu.VMEM((count, mid), F32),
            pltpu.VMEM((count, mid), F32),
            pltpu.VMEM((count, mid), F32),
            pltpu.VMEM((count, mid), F32),
        ],
        compiler_params=params(16),
        cost_estimate=pl.CostEstimate(
            flops=2 * 361 * count * mid * mid,
            bytes_accessed=8 * places * count * mid + 2 * weight.size,
            transcendentals=0,
        ),
    )(core, y, mine, other, onehot, gain, shift, weight)


def expand_kernel(
    rows,
    core_ref,
    z_ref,
    mine_ref,
    other_ref,
    p_ref,
    gain_ref,
    shift_ref,
    w_ref,
    act_ref,
    keep_ref,
    send_ref,
    scale_s,
    shift_s,
    s1,
    s2,
):
    step = pl.program_id(0)
    side, count, mid = z_ref.shape

    @pl.when(step == 0)
    def _():
        scale, shift = scale_shift(
            core_ref[0], mine_ref[...], other_ref[...], p_ref[...], gain_ref[...], shift_ref[...], rows
        )
        scale_s[...] = scale
        shift_s[...] = shift
        s1[...] = jnp.zeros_like(s1)
        s2[...] = jnp.zeros_like(s2)

    a = jnp.maximum(z_ref[...] * scale_s[...][None] + shift_s[...][None], 0.0).astype(BF16)
    act_ref[...] = a
    s1[...] += jnp.sum(a.astype(F32), 0)
    wide = dot32(a.reshape(side * count, mid), w_ref[...]).reshape(side, count, -1)
    s2[...] += jnp.sum(wide * wide, 0)

    @pl.when(step == pl.num_programs(0) - 1)
    def _():
        core = core_ref[0]
        onehot = p_ref[...]
        split_halves(core, pick_rows(onehot, s1[...]), keep_ref, send_ref, 0)
        split_halves(core, pick_rows(onehot, s2[...]), keep_ref, send_ref, mid // 2)


def expand_stage(rows, core, z, mine, other, onehot, gain, shift, weight):
    places, count, mid = z.shape
    wide = weight.shape[1]
    sums = (mid + wide) // 2
    return pl.pallas_call(
        functools.partial(expand_kernel, rows),
        name="expand",
        grid=(SIDE,),
        in_specs=[
            SMEM,
            pl.BlockSpec((SIDE, count, mid), lambda i: (i, 0, 0)),
            VMEM,
            VMEM,
            VMEM,
            VMEM,
            VMEM,
            VMEM,
        ],
        out_specs=[
            pl.BlockSpec((SIDE, count, mid), lambda i: (i, 0, 0)),
            pl.BlockSpec((count, sums), lambda i: (0, 0)),
            pl.BlockSpec((count, sums), lambda i: (0, 0)),
        ],
        out_shape=[
            jax.ShapeDtypeStruct((places, count, mid), BF16),
            jax.ShapeDtypeStruct((count, sums), F32),
            jax.ShapeDtypeStruct((count, sums), F32),
        ],
        scratch_shapes=[
            pltpu.VMEM((count, mid), F32),
            pltpu.VMEM((count, mid), F32),
            pltpu.VMEM((count, mid), F32),
            pltpu.VMEM((count, wide), F32),
        ],
        compiler_params=params(16),
        cost_estimate=pl.CostEstimate(
            flops=2 * places * count * mid * wide,
            bytes_accessed=6 * places * count * mid,
            transcendentals=0,
        ),
    )(core, z, mine, other, onehot, gain, shift, weight)


def merge_kernel(
    rows,
    core_ref,
    a_ref,
    x_ref,
    mine_ref,
    other_ref,
    p_ref,
    gain_ref,
    shift_ref,
    w_ref,
    proj_ref,
    key_ref,
    scale_s,
    shift_s,
    pool,
):
    step = pl.program_id(0)
    side, count, mid = a_ref.shape

    @pl.when(step == 0)
    def _():
        core, onehot = core_ref[0], p_ref[...]
        mine, other = mine_ref[...], other_ref[...]
        cut = mid // 2
        sums = join_halves(core, mine[:, :cut], other[:, :cut])
        squares = join_halves(core, mine[:, cut:], other[:, cut:])
        high = sums.astype(BF16)
        rest = sums - high.astype(F32)
        middle = rest.astype(BF16)
        low = (rest - middle.astype(F32)).astype(BF16)
        w = w_ref[...]
        average = (dot32(high, w) + (dot32(middle, w) + dot32(low, w))) / rows
        spread = squares / rows - average * average
        scale = lax.rsqrt(spread + EPS) * gain_ref[...]
        scale_s[...] = unpick_rows(onehot, scale)
        shift_s[...] = unpick_rows(onehot, shift_ref[...] - average * scale)
        pool[...] = jnp.zeros_like(pool)

    wide = dot32(a_ref[...].reshape(side * count, mid), w_ref[...]).reshape(side, count, -1)
    merged = jnp.maximum(
        wide * scale_s[...][None] + shift_s[...][None] + x_ref[...].astype(F32), 0.0
    )
    pool[...] += jnp.sum(merged, 0)

    @pl.when(step == pl.num_programs(0) - 1)
    def _():
        pooled = (pool[...] / (side * pl.num_programs(0))).astype(BF16)
        u = dot32(pooled, proj_ref[...])
        key_ref[...] = (u * lax.rsqrt(jnp.sum(u * u, 1, keepdims=True) + UNIT_EPS)).astype(BF16)


def merge_stage(rows, core, a, x, mine, other, onehot, gain, shift, weight, proj):
    places, count, mid = a.shape
    wide = weight.shape[1]
    feat = proj.shape[1]
    return pl.pallas_call(
        functools.partial(merge_kernel, rows),
        name="merge",
        grid=(SIDE,),
        in_specs=[
            SMEM,
            pl.BlockSpec((SIDE, count, mid), lambda i: (i, 0, 0)),
            pl.BlockSpec((SIDE, count, wide), lambda i: (i, 0, 0)),
            VMEM,
            VMEM,
            VMEM,
            VMEM,
            VMEM,
            VMEM,
            VMEM,
        ],
        out_specs=pl.BlockSpec((count, feat), lambda i: (0, 0)),
        out_shape=jax.ShapeDtypeStruct((count, feat), BF16),
        scratch_shapes=[
            pltpu.VMEM((count, wide), F32),
            pltpu.VMEM((count, wide), F32),
            pltpu.VMEM((count, wide), F32),
        ],
        compiler_params=params(16),
        cost_estimate=pl.CostEstimate(
            flops=2 * places * count * mid * wide,
            bytes_accessed=2 * x.size + 2 * a.size,
            transcendentals=0,
        ),
    )(core, a, x, mine, other, onehot, gain, shift, weight, proj)


def negative_kernel(factor, q_ref, k_ref, out_ref):
    @pl.when(pl.program_id(0) == 0)
    def _():
        out_ref[...] = jnp.zeros_like(out_ref)

    keys = k_ref[...]
    wide = keys.astype(F32)
    norm = lax.rsqrt(jnp.sum(wide * wide, 1, keepdims=True) + UNIT_EPS) * factor
    score = lax.dot_general(
        keys, q_ref[...], (((1,), (1,)), ((), ())), preferred_element_type=F32
    )
    out_ref[...] += jnp.sum(jnp.exp2(score * norm), 0, keepdims=True)


def negative_stage(queries, keys):
    count, feat = queries.shape
    total = keys.shape[0]
    block = math.gcd(total, 2048)
    return pl.pallas_call(
        functools.partial(negative_kernel, math.log2(math.e) / TEMP),
        name="negative",
        grid=(total // block,),
        in_specs=[VMEM, pl.BlockSpec((block, feat), lambda i: (i, 0))],
        out_specs=pl.BlockSpec((1, count), lambda i: (0, 0)),
        out_shape=jax.ShapeDtypeStruct((1, count), F32),
        compiler_params=params(8),
        cost_estimate=pl.CostEstimate(
            flops=2 * total * count * feat,
            bytes_accessed=2 * total * feat,
            transcendentals=total * count,
        ),
    )(queries, keys)


def loss_kernel(table_ref, u_ref, pos_ref, neg_ref, loss_ref):
    logits = lax.dot_general(
        table_ref[...], u_ref[...], (((1,), (1,)), ((), ())), preferred_element_type=F32
    )
    row = lax.broadcasted_iota(jnp.int32, logits.shape, 0)
    picked = jnp.sum(jnp.where(row == pos_ref[...], logits, 0.0), 0, keepdims=True) / TEMP
    loss_ref[...] = jnp.log(jnp.exp(picked) + neg_ref[...]) - picked


def loss_stage(table, units, positive, negatives):
    return pl.pallas_call(
        loss_kernel,
        name="loss",
        in_specs=[VMEM] * 4,
        out_specs=VMEM,
        out_shape=jax.ShapeDtypeStruct(positive.shape, F32),
        compiler_params=pltpu.CompilerParams(vmem_limit_bytes=8 * 1024 * 1024),
    )(table, units, positive, negatives)


def unit_rows(values):
    as_float = values.astype(F32)
    return (
        as_float * lax.rsqrt(jnp.sum(as_float * as_float, -1, keepdims=True) + UNIT_EPS)
    ).astype(BF16)


RING = 4


def swap_core():
    return [(i, i ^ 1) for i in range(2 * RING * RING)]


def ring_shift(k, flip):
    pairs = []
    for i in range(2 * RING * RING):
        x, z, c = i // (2 * RING), (i // 2) % RING, i % 2
        if (c == 1) != flip:
            x = (x + k) % RING
        else:
            z = (z + k) % RING
        pairs.append((i, (x * RING + z) * 2 + c))
    return pairs


def reduce_sets(keep, send):
    total = keep + lax.ppermute(send, "dp", swap_core())
    for flip in (False, True):
        parts = [lax.ppermute(total, "dp", ring_shift(k, flip)) for k in (1, 2, 3)]
        total = (total + parts[0]) + (parts[1] + parts[2])
    return total, lax.ppermute(total, "dp", swap_core())


def on_device(
    features,
    shuffle,
    positive,
    queries,
    queue_keys,
    reduce_weight,
    gain_one,
    shift_one,
    w_spatial,
    gain_two,
    shift_two,
    w_expand,
    gain_three,
    shift_three,
    w_project,
):
    count, places, channels = features.shape
    peers = lax.axis_size("dp")
    groups = lax.axis_size("queue")
    me = lax.axis_index("dp")
    core = jnp.bitwise_and(me, 1).astype(jnp.int32).reshape(1)
    rows = count * places
    x = jnp.transpose(features, (1, 0, 2))
    sets = shuffle.reshape(peers, count, 1)
    local = (me * count + jnp.arange(count, dtype=jnp.int32)).reshape(1, 1, count)
    onehot = jnp.any(sets == local, 1).astype(F32)

    units = unit_rows(queries)
    around = [(i, (i + k) % groups) for k in range(groups) for i in range(groups)]
    gathered = [units] + [
        lax.ppermute(units, "queue", around[k * groups : (k + 1) * groups])
        for k in range(1, groups)
    ]
    y, keep, send = reduce_stage(core, x, reduce_weight, onehot)
    mine, other = reduce_sets(keep, send)
    partial = negative_stage(jnp.concatenate(gathered, 0), queue_keys)
    z, keep, send = conv_stage(
        rows, core, y, mine, other, onehot, gain_one[None], shift_one[None], w_spatial
    )
    mine, other = reduce_sets(keep, send)
    negatives = partial[:, :count]
    for k in range(1, groups):
        back = groups - k
        negatives = negatives + lax.ppermute(
            partial[:, k * count : (k + 1) * count],
            "queue",
            around[back * groups : (back + 1) * groups],
        )
    act, keep, send = expand_stage(
        rows, core, z, mine, other, onehot, gain_two[None], shift_two[None], w_expand
    )
    mine, other = reduce_sets(keep, send)
    key_rows = merge_stage(
        rows,
        core,
        act,
        x,
        mine,
        other,
        onehot,
        gain_three[None],
        shift_three[None],
        w_expand,
        w_project,
    )
    copies = jnp.broadcast_to(key_rows[None], (peers,) + key_rows.shape)
    table = lax.all_to_all(copies, "dp", split_axis=0, concat_axis=0, tiled=True)
    table = table.reshape(peers * count, -1)
    loss_vals = loss_stage(table, units, positive.reshape(1, count), negatives)
    return (loss_vals.reshape(count), key_rows)


def solution(mesh):
    placed = (
        P(("queue", "dp"), None, None),
        P("queue", None),
        P(("queue", "dp")),
        P(("queue", "dp"), None),
        P("queue", None),
    ) + (P(),) * 10
    return jax.shard_map(
        on_device,
        mesh=mesh,
        in_specs=placed,
        out_specs=(P(("queue", "dp")), P(("queue", "dp"), None)),
        check_vma=False,
    )
```

```python
import functools
import math

import jax
import jax.numpy as jnp
from jax import lax
from jax.experimental import pallas as pl
from jax.experimental.pallas import tpu as pltpu
from jax.sharding import PartitionSpec as P

SIDE = 7
EPS = 1e-05
UNIT_EPS = 1e-06
TEMP = 0.2
HIGH = lax.Precision.HIGHEST
F32 = jnp.float32
BF16 = jnp.bfloat16
VMEM = pl.BlockSpec(memory_space=pltpu.VMEM)
SMEM = pl.BlockSpec(memory_space=pltpu.SMEM)


def params(limit_mib):
    return pltpu.CompilerParams(
        dimension_semantics=("arbitrary",), vmem_limit_bytes=limit_mib * 1024 * 1024
    )


def dot32(a, b):
    return jnp.dot(a, b, preferred_element_type=F32)


def pick_rows(onehot, values):
    return lax.dot_general(
        onehot, values, (((0,), (0,)), ((), ())), precision=HIGH, preferred_element_type=F32
    )


def unpick_rows(onehot, values):
    return lax.dot_general(
        onehot, values, (((1,), (0,)), ((), ())), precision=HIGH, preferred_element_type=F32
    )


def set_onehot(me, shuffle, count):
    total = shuffle.shape[1]
    image = lax.broadcasted_iota(jnp.int32, (count, total), 0) + me * count
    here = (shuffle == image).astype(F32)
    slot = lax.broadcasted_iota(jnp.int32, (total, total // count), 0)
    member = lax.broadcasted_iota(jnp.int32, (total, total // count), 1)
    low = member * count
    inside = jnp.logical_and(slot >= low, slot < low + count)
    return dot32(here.astype(BF16), inside.astype(F32).astype(BF16))


def split_halves(core, values, keep_ref, send_ref, start):
    half = values.shape[1] // 2
    low, high = values[:, :half], values[:, half:]
    keep_ref[:, start : start + half] = jnp.where(core == 0, low, high)
    send_ref[:, start : start + half] = jnp.where(core == 0, high, low)


def join_halves(core, mine, other):
    low = jnp.where(core == 0, mine, other)
    high = jnp.where(core == 0, other, mine)
    return jnp.concatenate([low, high], 1)


CHUNKS = ((0, 7), (7, 14), (21, 28))


def reduce_kernel(
    me_ref, x_hbm, w_hbm, shuffle_ref, y_ref, keep_ref, send_ref, p_ref, x_ref, w_ref, sems
):
    places, count, channels = x_ref.shape
    mid = w_ref.shape[1]
    weight_copy = pltpu.make_async_copy(w_hbm, w_ref, sems.at[0])
    weight_copy.start()
    copies = []
    for n, (first, size) in enumerate(CHUNKS):
        part = pl.ds(first, size)
        copies.append(pltpu.make_async_copy(x_hbm.at[part], x_ref.at[part], sems.at[n + 1]))
        copies[-1].start()
    onehot = set_onehot(me_ref[0], shuffle_ref[...], count)
    p_ref[...] = onehot
    weight_copy.wait()
    s1 = jnp.zeros((count, mid), F32)
    s2 = jnp.zeros((count, mid), F32)
    for (first, size), copy in zip(CHUNKS, copies):
        copy.wait()
        part = pl.ds(first, size)
        y = dot32(x_ref[part].reshape(size * count, channels), w_ref[...])
        y = y.reshape(size, count, mid)
        y_ref[part] = y
        s1 += jnp.sum(y, 0)
        s2 += jnp.sum(y * y, 0)
    core = jnp.bitwise_and(me_ref[0], 1)
    split_halves(core, pick_rows(onehot, s1), keep_ref, send_ref, 0)
    split_halves(core, pick_rows(onehot, s2), keep_ref, send_ref, mid // 2)


def reduce_stage(me, x, weight, shuffle):
    places, count, channels = x.shape
    mid = weight.shape[1]
    sets = shuffle.shape[1] // count
    hbm = pl.BlockSpec(memory_space=pltpu.HBM)
    return pl.pallas_call(
        reduce_kernel,
        name="reduce",
        in_specs=[SMEM, hbm, hbm, VMEM],
        out_specs=[VMEM] * 5,
        out_shape=[
            jax.ShapeDtypeStruct((places, count, mid), F32),
            jax.ShapeDtypeStruct((count, mid), F32),
            jax.ShapeDtypeStruct((count, mid), F32),
            jax.ShapeDtypeStruct((count, sets), F32),
            jax.ShapeDtypeStruct(x.shape, x.dtype),
        ],
        scratch_shapes=[
            pltpu.VMEM(weight.shape, weight.dtype),
            pltpu.SemaphoreType.DMA((len(CHUNKS) + 1,)),
        ],
        compiler_params=pltpu.CompilerParams(vmem_limit_bytes=24 * 1024 * 1024),
        cost_estimate=pl.CostEstimate(
            flops=2 * places * count * channels * mid,
            bytes_accessed=2 * x.size + 4 * places * count * mid,
            transcendentals=0,
        ),
    )(me, pltpu.with_memory_space_constraint(x, pltpu.HBM), pltpu.with_memory_space_constraint(weight, pltpu.HBM), shuffle)


def scale_shift(core, mine, other, onehot, gain, shift, rows):
    half = mine.shape[1] // 2
    total1 = join_halves(core, mine[:, :half], other[:, :half])
    total2 = join_halves(core, mine[:, half:], other[:, half:])
    average = total1 / rows
    spread = total2 / rows - average * average
    scale = lax.rsqrt(spread + EPS) * gain
    return unpick_rows(onehot, scale), unpick_rows(onehot, shift - average * scale)


def conv_kernel(
    rows,
    core_ref,
    y_ref,
    mine_ref,
    other_ref,
    p_ref,
    gain_ref,
    shift_ref,
    w_ref,
    z_ref,
    keep_ref,
    send_ref,
    act,
    scale_s,
    shift_s,
    s1,
    s2,
):
    step = pl.program_id(0)
    side = SIDE
    _, count, mid = y_ref.shape

    def norm(row):
        a = y_ref[pl.ds(row * side, side)] * scale_s[...][None] + shift_s[...][None]
        act[row] = jnp.maximum(a, 0.0).astype(BF16)

    def conv_row(row, dys):
        for dx in (0, -1, 1):
            lo, hi = max(0, -dx), side - max(0, dx)
            window = [act[row + dy, lo + dx : hi + dx].reshape((hi - lo) * count, mid) for dy in dys]
            weight = [w_ref[3 * (dy + 1) + dx + 1] for dy in dys]
            part = dot32(jnp.concatenate(window, 1), jnp.concatenate(weight, 0))
            part = part.reshape(hi - lo, count, mid)
            if dx == 0:
                z_ref[pl.ds(row * side, side)] = part
            else:
                z_ref[pl.ds(row * side + lo, hi - lo)] += part
        z = z_ref[pl.ds(row * side, side)]
        s1[...] += jnp.sum(z, 0)
        s2[...] += jnp.sum(z * z, 0)

    @pl.when(step == 0)
    def _():
        scale, shift = scale_shift(
            core_ref[0], mine_ref[...], other_ref[...], p_ref[...], gain_ref[...], shift_ref[...], rows
        )
        scale_s[...] = scale
        shift_s[...] = shift
        s1[...] = jnp.zeros_like(s1)
        s2[...] = jnp.zeros_like(s2)
        norm(0)
        norm(1)
        conv_row(0, (0, 1))
        norm(2)

    @pl.when(jnp.logical_and(step > 0, step < side - 1))
    def _():
        conv_row(step, (-1, 0, 1))
        norm(jnp.minimum(step + 2, side - 1))

    @pl.when(step == side - 1)
    def _():
        conv_row(side - 1, (-1, 0))
        core = core_ref[0]
        onehot = p_ref[...]
        split_halves(core, pick_rows(onehot, s1[...]), keep_ref, send_ref, 0)
        split_halves(core, pick_rows(onehot, s2[...]), keep_ref, send_ref, mid // 2)


def conv_stage(rows, core, y, mine, other, onehot, gain, shift, weight):
    places, count, mid = y.shape
    return pl.pallas_call(
        functools.partial(conv_kernel, rows),
        name="conv",
        grid=(SIDE,),
        in_specs=[SMEM] + [VMEM] * 7,
        out_specs=[VMEM] * 3,
        out_shape=[
            jax.ShapeDtypeStruct((places, count, mid), F32),
            jax.ShapeDtypeStruct((count, mid), F32),
            jax.ShapeDtypeStruct((count, mid), F32),
        ],
        scratch_shapes=[
            pltpu.VMEM((SIDE, SIDE, count, mid), BF16),
            pltpu.VMEM((count, mid), F32),
            pltpu.VMEM((count, mid), F32),
            pltpu.VMEM((count, mid), F32),
            pltpu.VMEM((count, mid), F32),
        ],
        compiler_params=params(16),
        cost_estimate=pl.CostEstimate(
            flops=2 * 361 * count * mid * mid,
            bytes_accessed=8 * places * count * mid + 2 * weight.size,
            transcendentals=0,
        ),
    )(core, y, mine, other, onehot, gain, shift, weight)


COLUMNS = 256


def expand_kernel(
    rows,
    core_ref,
    z_ref,
    mine_ref,
    other_ref,
    p_ref,
    gain_ref,
    shift_ref,
    w_ref,
    act_ref,
    keep_ref,
    send_ref,
    sq_s,
):
    places, count, mid = z_ref.shape
    wide = w_ref.shape[1]
    core = core_ref[0]
    onehot = p_ref[...]
    scale, shift = scale_shift(
        core, mine_ref[...], other_ref[...], onehot, gain_ref[...], shift_ref[...], rows
    )
    total = jnp.zeros((count, mid), F32)
    for row in range(0, places, SIDE):
        a = z_ref[row : row + SIDE] * scale[None] + shift[None]
        a = jnp.maximum(a, 0.0).astype(BF16)
        act_ref[row : row + SIDE] = a
        total += jnp.sum(a.astype(F32), 0)
    flat = act_ref[...].reshape(places * count, mid)
    for j in range(0, wide, COLUMNS):
        e = dot32(flat, w_ref[:, j : j + COLUMNS]).reshape(places, count, COLUMNS)
        sq_s[:, j : j + COLUMNS] = jnp.sum(e * e, 0)
    split_halves(core, pick_rows(onehot, total), keep_ref, send_ref, 0)
    split_halves(core, pick_rows(onehot, sq_s[...]), keep_ref, send_ref, mid // 2)


def expand_stage(rows, core, z, mine, other, onehot, gain, shift, weight):
    places, count, mid = z.shape
    wide = weight.shape[1]
    sums = (mid + wide) // 2
    return pl.pallas_call(
        functools.partial(expand_kernel, rows),
        name="expand",
        in_specs=[SMEM] + [VMEM] * 7,
        out_specs=[VMEM] * 3,
        out_shape=[
            jax.ShapeDtypeStruct((places, count, mid), BF16),
            jax.ShapeDtypeStruct((count, sums), F32),
            jax.ShapeDtypeStruct((count, sums), F32),
        ],
        scratch_shapes=[pltpu.VMEM((count, wide), F32)],
        compiler_params=pltpu.CompilerParams(vmem_limit_bytes=16 * 1024 * 1024),
        cost_estimate=pl.CostEstimate(
            flops=2 * places * count * mid * wide,
            bytes_accessed=6 * places * count * mid,
            transcendentals=0,
        ),
    )(core, z, mine, other, onehot, gain, shift, weight)


def merge_kernel(
    rows,
    core_ref,
    a_ref,
    x_ref,
    mine_ref,
    other_ref,
    p_ref,
    gain_ref,
    shift_ref,
    w_ref,
    proj_ref,
    key_ref,
    copies_ref,
    scale_s,
    shift_s,
    pool,
):
    places, count, mid = a_ref.shape
    wide = w_ref.shape[1]
    core, onehot = core_ref[0], p_ref[...]
    mine, other = mine_ref[...], other_ref[...]
    cut = mid // 2
    sums = join_halves(core, mine[:, :cut], other[:, :cut])
    squares = join_halves(core, mine[:, cut:], other[:, cut:])
    high = sums.astype(BF16)
    rest = sums - high.astype(F32)
    middle = rest.astype(BF16)
    low = (rest - middle.astype(F32)).astype(BF16)
    three = dot32(jnp.concatenate([high, middle, low], 0), w_ref[...])
    sets = sums.shape[0]
    average = (three[:sets] + (three[sets : 2 * sets] + three[2 * sets :])) / rows
    spread = squares / rows - average * average
    scale = lax.rsqrt(spread + EPS) * gain_ref[...]
    scale_s[...] = unpick_rows(onehot, scale)
    shift_s[...] = unpick_rows(onehot, shift_ref[...] - average * scale)
    flat = a_ref[...].reshape(places * count, mid)
    for j in range(0, wide, COLUMNS):
        cols = slice(j, j + COLUMNS)
        e = dot32(flat, w_ref[:, cols]).reshape(places, count, COLUMNS)
        sc, sh = scale_s[:, cols], shift_s[:, cols]
        total = jnp.zeros((count, COLUMNS), F32)
        for place in range(places):
            total += jnp.maximum(e[place] * sc + sh + x_ref[place, :, cols].astype(F32), 0.0)
        pool[:, cols] = total
    pooled = (pool[...] / places).astype(BF16)
    u = dot32(pooled, proj_ref[...])
    key = (u * lax.rsqrt(jnp.sum(u * u, 1, keepdims=True) + UNIT_EPS)).astype(BF16)
    key_ref[...] = key
    copies_ref[...] = jnp.broadcast_to(key[None], copies_ref.shape)


def merge_stage(rows, core, peers, a, x, mine, other, onehot, gain, shift, weight, proj):
    places, count, mid = a.shape
    wide = weight.shape[1]
    feat = proj.shape[1]
    return pl.pallas_call(
        functools.partial(merge_kernel, rows),
        name="merge",
        in_specs=[SMEM] + [VMEM] * 9,
        out_specs=[VMEM] * 2,
        out_shape=[
            jax.ShapeDtypeStruct((count, feat), BF16),
            jax.ShapeDtypeStruct((peers, count, feat), BF16),
        ],
        scratch_shapes=[
            pltpu.VMEM((count, wide), F32),
            pltpu.VMEM((count, wide), F32),
            pltpu.VMEM((count, wide), F32),
        ],
        compiler_params=pltpu.CompilerParams(vmem_limit_bytes=16 * 1024 * 1024),
        cost_estimate=pl.CostEstimate(
            flops=2 * places * count * mid * wide,
            bytes_accessed=2 * x.size + 2 * a.size,
            transcendentals=0,
        ),
    )(core, a, x, mine, other, onehot, gain, shift, weight, proj)


def negative_kernel(factor, q_ref, k_ref, out_ref):
    @pl.when(pl.program_id(0) == 0)
    def _():
        out_ref[...] = jnp.zeros_like(out_ref)

    keys = k_ref[...]
    wide = keys.astype(F32)
    norm = lax.rsqrt(jnp.sum(wide * wide, 1, keepdims=True) + UNIT_EPS) * factor
    score = lax.dot_general(
        keys, q_ref[...], (((1,), (1,)), ((), ())), preferred_element_type=F32
    )
    out_ref[...] += jnp.sum(jnp.exp2(score * norm), 0, keepdims=True)


def negative_stage(queries, keys, part, parts):
    count, feat = queries.shape
    total = keys.shape[0] // parts
    block = math.gcd(total, 2048)
    steps = total // block
    return pl.pallas_call(
        functools.partial(negative_kernel, math.log2(math.e) / TEMP),
        name="negative",
        grid=(steps,),
        in_specs=[VMEM, pl.BlockSpec((block, feat), lambda i: (i + part * steps, 0))],
        out_specs=pl.BlockSpec((1, count), lambda i: (0, 0)),
        out_shape=jax.ShapeDtypeStruct((1, count), F32),
        compiler_params=params(8),
        cost_estimate=pl.CostEstimate(
            flops=2 * total * count * feat,
            bytes_accessed=2 * total * feat,
            transcendentals=total * count,
        ),
    )(queries, keys)


def loss_kernel(table_ref, u_ref, pos_ref, neg_ref, loss_ref):
    logits = lax.dot_general(
        table_ref[...], u_ref[...], (((1,), (1,)), ((), ())), preferred_element_type=F32
    )
    row = lax.broadcasted_iota(jnp.int32, logits.shape, 0)
    picked = jnp.sum(jnp.where(row == pos_ref[...], logits, 0.0), 0, keepdims=True) / TEMP
    loss_ref[...] = jnp.log(jnp.exp(picked) + neg_ref[...]) - picked


def loss_stage(table, units, positive, negatives):
    return pl.pallas_call(
        loss_kernel,
        name="loss",
        in_specs=[VMEM] * 4,
        out_specs=VMEM,
        out_shape=jax.ShapeDtypeStruct(positive.shape, F32),
        compiler_params=pltpu.CompilerParams(vmem_limit_bytes=8 * 1024 * 1024),
    )(table, units, positive, negatives)


def unit_rows(values):
    as_float = values.astype(F32)
    return (
        as_float * lax.rsqrt(jnp.sum(as_float * as_float, -1, keepdims=True) + UNIT_EPS)
    ).astype(BF16)


RING = 4


def swap_core():
    return [(i, i ^ 1) for i in range(2 * RING * RING)]


def ring_swap(k, flip):
    pairs = []
    for i in range(2 * RING * RING):
        x, z, c = i // (2 * RING), (i // 2) % RING, i % 2
        if (c == 1) != flip:
            x = x ^ k
        else:
            z = z ^ k
        pairs.append((i, (x * RING + z) * 2 + c))
    return pairs


def queue_swap(values, k):
    return lax.ppermute(values, "queue", [(i, i ^ k) for i in range(RING)])


def reduce_sets(keep, send, side_work, side_input):
    total = keep + lax.ppermute(send, "dp", swap_core())
    for flip, work in zip((False, True), side_work):
        parts = [lax.ppermute(total, "dp", ring_swap(k, flip)) for k in (1, 2, 3)]
        side_input, _ = lax.optimization_barrier((side_input, total))
        side_input = work(side_input)
        parts, side_input = lax.optimization_barrier((parts, side_input))
        total = (total + parts[0]) + (parts[1] + parts[2])
    return total, lax.ppermute(total, "dp", swap_core()), side_input


def on_device(
    features,
    shuffle,
    positive,
    queries,
    queue_keys,
    reduce_weight,
    gain_one,
    shift_one,
    w_spatial,
    gain_two,
    shift_two,
    w_expand,
    gain_three,
    shift_three,
    w_project,
):
    count, places, channels = features.shape
    peers = lax.axis_size("dp")
    me = lax.axis_index("dp").astype(jnp.int32).reshape(1)
    core = jnp.bitwise_and(me, 1)
    rows = count * places
    x = jnp.transpose(features, (1, 0, 2))
    units = unit_rows(queries)

    def gather_one(own):
        return jnp.concatenate([own, queue_swap(own, 1)], 0)

    def gather_two(pair):
        return jnp.concatenate([pair, queue_swap(pair, 3)], 0)

    def negative_one(queries_here):
        return queries_here, negative_stage(queries_here, queue_keys, 0, 2)

    def negative_two(state):
        return state[1] + negative_stage(state[0], queue_keys, 1, 2)

    def return_one(sums):
        return sums[:, : 2 * count] + queue_swap(sums[:, 2 * count :], 3)

    def return_two(sums):
        return sums[:, :count] + queue_swap(sums[:, count:], 1)

    y, keep, send, onehot, x = reduce_stage(me, x, reduce_weight, shuffle)
    mine, other, gathered = reduce_sets(keep, send, (gather_one, gather_two), units)
    z, keep, send = conv_stage(
        rows, core, y, mine, other, onehot, gain_one[None], shift_one[None], w_spatial
    )
    mine, other, sums = reduce_sets(keep, send, (negative_one, negative_two), gathered)
    act, keep, send = expand_stage(
        rows, core, z, mine, other, onehot, gain_two[None], shift_two[None], w_expand
    )
    mine, other, negatives = reduce_sets(keep, send, (return_one, return_two), sums)
    key_rows, copies = merge_stage(
        rows,
        core,
        peers,
        act,
        x,
        mine,
        other,
        onehot,
        gain_three[None],
        shift_three[None],
        w_expand,
        w_project,
    )
    table = lax.all_to_all(copies, "dp", split_axis=0, concat_axis=0, tiled=True)
    table = table.reshape(peers * count, -1)
    loss_vals = loss_stage(table, units, positive.reshape(1, count), negatives)
    return (loss_vals.reshape(count), key_rows)


def solution(mesh):
    placed = (
        P(("queue", "dp"), None, None),
        P("queue", None),
        P(("queue", "dp")),
        P(("queue", "dp"), None),
        P("queue", None),
    ) + (P(),) * 10
    return jax.shard_map(
        on_device,
        mesh=mesh,
        in_specs=placed,
        out_specs=(P(("queue", "dp")), P(("queue", "dp"), None)),
        check_vma=False,
    )
```

```python
import functools
import math

import jax
import jax.numpy as jnp
from jax import lax
from jax.experimental import pallas as pl
from jax.experimental.pallas import tpu as pltpu
from jax.sharding import PartitionSpec as P

SIDE = 7
EPS = 1e-05
UNIT_EPS = 1e-06
TEMP = 0.2
HIGH = lax.Precision.HIGHEST
F32 = jnp.float32
BF16 = jnp.bfloat16
VMEM = pl.BlockSpec(memory_space=pltpu.VMEM)
SMEM = pl.BlockSpec(memory_space=pltpu.SMEM)


def params(limit_mib):
    return pltpu.CompilerParams(
        dimension_semantics=("arbitrary",), vmem_limit_bytes=limit_mib * 1024 * 1024
    )


def dot32(a, b):
    return jnp.dot(a, b, preferred_element_type=F32)


def pieces(values):
    high = values.astype(BF16)
    rest = values - high.astype(F32)
    middle = rest.astype(BF16)
    low = (rest - middle.astype(F32)).astype(BF16)
    return jnp.concatenate([high, middle, low], 0)


def set_onehots(me, shuffle, count):
    total = shuffle.shape[1]
    image = lax.broadcasted_iota(jnp.int32, (count, total), 0) + me * count
    here = (shuffle == image).astype(F32)
    slot = lax.broadcasted_iota(jnp.int32, (total, total // count), 0)
    low = lax.broadcasted_iota(jnp.int32, (total, total // count), 1) * count
    inside = jnp.logical_and(slot >= low, slot < low + count)
    by_image = dot32(here.astype(BF16), inside.astype(F32).astype(BF16))
    by_set = jnp.transpose(by_image, (1, 0))
    return [jnp.concatenate([p] * 3, 1).astype(BF16) for p in (by_set, by_image)]


def reorder(onehot, values):
    return dot32(onehot, pieces(values))


def split_halves(core, values, keep_ref, send_ref, start):
    half = values.shape[1] // 2
    low, high = values[:, :half], values[:, half:]
    keep_ref[:, start : start + half] = jnp.where(core == 0, low, high)
    send_ref[:, start : start + half] = jnp.where(core == 0, high, low)


def join_halves(core, mine, other):
    low = jnp.where(core == 0, mine, other)
    high = jnp.where(core == 0, other, mine)
    return jnp.concatenate([low, high], 1)


CHUNKS = ((0, 7), (7, 14), (21, 28))


def reduce_kernel(
    me_ref,
    x_hbm,
    w_hbm,
    shuffle_hbm,
    y_ref,
    keep_ref,
    send_ref,
    by_set_ref,
    by_image_ref,
    x_ref,
    w_ref,
    shuffle_ref,
    sems,
):
    places, count, channels = x_ref.shape
    mid = w_ref.shape[1]
    weight_copy = pltpu.make_async_copy(w_hbm, w_ref, sems.at[0])
    weight_copy.start()
    copies = []
    for n, (first, size) in enumerate(CHUNKS):
        part = pl.ds(first, size)
        copies.append(pltpu.make_async_copy(x_hbm.at[part], x_ref.at[part], sems.at[n + 1]))
        copies[-1].start()
    shuffle_copy = pltpu.make_async_copy(shuffle_hbm, shuffle_ref, sems.at[len(CHUNKS) + 1])
    shuffle_copy.start()
    shuffle_copy.wait()
    by_set, by_image = set_onehots(me_ref[0], shuffle_ref[...], count)
    by_set_ref[...] = by_set
    by_image_ref[...] = by_image
    weight_copy.wait()
    s1 = jnp.zeros((count, mid), F32)
    s2 = jnp.zeros((count, mid), F32)
    for (first, size), copy in zip(CHUNKS, copies):
        copy.wait()
        part = pl.ds(first, size)
        y = dot32(x_ref[part].reshape(size * count, channels), w_ref[...])
        y = y.reshape(size, count, mid)
        y_ref[part] = y
        s1 += jnp.sum(y, 0)
        s2 += jnp.sum(y * y, 0)
    core = jnp.bitwise_and(me_ref[0], 1)
    split_halves(core, reorder(by_set, s1), keep_ref, send_ref, 0)
    split_halves(core, reorder(by_set, s2), keep_ref, send_ref, mid // 2)


def reduce_stage(me, x, weight, shuffle):
    places, count, channels = x.shape
    mid = weight.shape[1]
    sets = shuffle.shape[1] // count
    hbm = pl.BlockSpec(memory_space=pltpu.HBM)
    return pl.pallas_call(
        reduce_kernel,
        name="reduce",
        in_specs=[SMEM, hbm, hbm, hbm],
        out_specs=[VMEM] * 6,
        out_shape=[
            jax.ShapeDtypeStruct((places, count, mid), F32),
            jax.ShapeDtypeStruct((count, mid), F32),
            jax.ShapeDtypeStruct((count, mid), F32),
            jax.ShapeDtypeStruct((sets, 3 * count), BF16),
            jax.ShapeDtypeStruct((count, 3 * sets), BF16),
            jax.ShapeDtypeStruct(x.shape, x.dtype),
        ],
        scratch_shapes=[
            pltpu.VMEM(weight.shape, weight.dtype),
            pltpu.VMEM(shuffle.shape, shuffle.dtype),
            pltpu.SemaphoreType.DMA((len(CHUNKS) + 2,)),
        ],
        compiler_params=pltpu.CompilerParams(vmem_limit_bytes=24 * 1024 * 1024),
        cost_estimate=pl.CostEstimate(
            flops=2 * places * count * channels * mid,
            bytes_accessed=2 * x.size + 4 * places * count * mid,
            transcendentals=0,
        ),
    )(me, *[pltpu.with_memory_space_constraint(v, pltpu.HBM) for v in (x, weight, shuffle)])


def scale_shift(core, mine, other, onehot, gain, shift, rows):
    half = mine.shape[1] // 2
    total1 = join_halves(core, mine[:, :half], other[:, :half])
    total2 = join_halves(core, mine[:, half:], other[:, half:])
    average = total1 / rows
    spread = total2 / rows - average * average
    scale = lax.rsqrt(spread + EPS) * gain
    return reorder(onehot, scale), reorder(onehot, shift - average * scale)


def conv_kernel(
    rows,
    core_ref,
    y_ref,
    mine_ref,
    other_ref,
    by_set_ref,
    by_image_ref,
    gain_ref,
    shift_ref,
    w_ref,
    z_ref,
    keep_ref,
    send_ref,
    act,
    scale_s,
    shift_s,
    s1,
    s2,
):
    step = pl.program_id(0)
    side = SIDE
    _, count, mid = y_ref.shape

    def norm(row):
        a = y_ref[pl.ds(row * side, side)] * scale_s[...][None] + shift_s[...][None]
        act[row] = jnp.maximum(a, 0.0).astype(BF16)

    def conv_row(row, dys):
        for dx in (0, -1, 1):
            lo, hi = max(0, -dx), side - max(0, dx)
            window = [act[row + dy, lo + dx : hi + dx].reshape((hi - lo) * count, mid) for dy in dys]
            weight = [w_ref[3 * (dy + 1) + dx + 1] for dy in dys]
            part = dot32(jnp.concatenate(window, 1), jnp.concatenate(weight, 0))
            part = part.reshape(hi - lo, count, mid)
            if dx == 0:
                z_ref[pl.ds(row * side, side)] = part
            else:
                z_ref[pl.ds(row * side + lo, hi - lo)] += part
        z = z_ref[pl.ds(row * side, side)]
        s1[...] += jnp.sum(z, 0)
        s2[...] += jnp.sum(z * z, 0)

    @pl.when(step == 0)
    def _():
        scale, shift = scale_shift(
            core_ref[0],
            mine_ref[...],
            other_ref[...],
            by_image_ref[...],
            gain_ref[...],
            shift_ref[...],
            rows,
        )
        scale_s[...] = scale
        shift_s[...] = shift
        s1[...] = jnp.zeros_like(s1)
        s2[...] = jnp.zeros_like(s2)
        norm(0)
        norm(1)
        conv_row(0, (0, 1))
        norm(2)

    @pl.when(jnp.logical_and(step > 0, step < side - 1))
    def _():
        conv_row(step, (-1, 0, 1))
        norm(jnp.minimum(step + 2, side - 1))

    @pl.when(step == side - 1)
    def _():
        conv_row(side - 1, (-1, 0))
        core = core_ref[0]
        by_set = by_set_ref[...]
        split_halves(core, reorder(by_set, s1[...]), keep_ref, send_ref, 0)
        split_halves(core, reorder(by_set, s2[...]), keep_ref, send_ref, mid // 2)


def conv_stage(rows, core, y, mine, other, by_set, by_image, gain, shift, weight):
    places, count, mid = y.shape
    return pl.pallas_call(
        functools.partial(conv_kernel, rows),
        name="conv",
        grid=(SIDE,),
        in_specs=[SMEM] + [VMEM] * 8,
        out_specs=[VMEM] * 3,
        out_shape=[
            jax.ShapeDtypeStruct((places, count, mid), F32),
            jax.ShapeDtypeStruct((count, mid), F32),
            jax.ShapeDtypeStruct((count, mid), F32),
        ],
        scratch_shapes=[
            pltpu.VMEM((SIDE, SIDE, count, mid), BF16),
            pltpu.VMEM((count, mid), F32),
            pltpu.VMEM((count, mid), F32),
            pltpu.VMEM((count, mid), F32),
            pltpu.VMEM((count, mid), F32),
        ],
        compiler_params=params(16),
        cost_estimate=pl.CostEstimate(
            flops=2 * 361 * count * mid * mid,
            bytes_accessed=8 * places * count * mid + 2 * weight.size,
            transcendentals=0,
        ),
    )(core, y, mine, other, by_set, by_image, gain, shift, weight)


COLUMNS = 256


def expand_kernel(
    rows,
    core_ref,
    z_ref,
    mine_ref,
    other_ref,
    by_set_ref,
    by_image_ref,
    gain_ref,
    shift_ref,
    w_ref,
    e_ref,
    keep_ref,
    send_ref,
    act,
    sq_s,
):
    places, count, mid = z_ref.shape
    wide = w_ref.shape[1]
    core = core_ref[0]
    by_set = by_set_ref[...]
    scale, shift = scale_shift(
        core,
        mine_ref[...],
        other_ref[...],
        by_image_ref[...],
        gain_ref[...],
        shift_ref[...],
        rows,
    )
    total = jnp.zeros((count, mid), F32)
    for row in range(0, places, SIDE):
        a = z_ref[row : row + SIDE] * scale[None] + shift[None]
        a = jnp.maximum(a, 0.0).astype(BF16)
        act[row : row + SIDE] = a
        total += jnp.sum(a.astype(F32), 0)
    flat = act[...].reshape(places * count, mid)
    for j in range(0, wide, COLUMNS):
        e = dot32(flat, w_ref[:, j : j + COLUMNS]).reshape(places, count, COLUMNS)
        e_ref[:, :, j : j + COLUMNS] = e
        sq_s[:, j : j + COLUMNS] = jnp.sum(e * e, 0)
    split_halves(core, reorder(by_set, total), keep_ref, send_ref, 0)
    split_halves(core, reorder(by_set, sq_s[...]), keep_ref, send_ref, mid // 2)


def expand_stage(rows, core, z, mine, other, by_set, by_image, gain, shift, weight):
    places, count, mid = z.shape
    wide = weight.shape[1]
    sums = (mid + wide) // 2
    return pl.pallas_call(
        functools.partial(expand_kernel, rows),
        name="expand",
        in_specs=[SMEM] + [VMEM] * 8,
        out_specs=[VMEM] * 3,
        out_shape=[
            jax.ShapeDtypeStruct((places, count, wide), F32),
            jax.ShapeDtypeStruct((count, sums), F32),
            jax.ShapeDtypeStruct((count, sums), F32),
        ],
        scratch_shapes=[
            pltpu.VMEM((places, count, mid), BF16),
            pltpu.VMEM((count, wide), F32),
        ],
        compiler_params=pltpu.CompilerParams(vmem_limit_bytes=16 * 1024 * 1024),
        cost_estimate=pl.CostEstimate(
            flops=2 * places * count * mid * wide,
            bytes_accessed=4 * places * count * (mid + wide),
            transcendentals=0,
        ),
    )(core, z, mine, other, by_set, by_image, gain, shift, weight)


def merge_kernel(
    rows,
    core_ref,
    e_ref,
    x_ref,
    mine_ref,
    other_ref,
    by_image_ref,
    gain_ref,
    shift_ref,
    w_ref,
    proj_ref,
    key_ref,
    copies_ref,
    scale_s,
    shift_s,
    pool,
):
    places, count, wide = e_ref.shape
    core, by_image = core_ref[0], by_image_ref[...]
    mine, other = mine_ref[...], other_ref[...]
    cut = w_ref.shape[0] // 2
    sums = join_halves(core, mine[:, :cut], other[:, :cut])
    squares = join_halves(core, mine[:, cut:], other[:, cut:])
    three = dot32(pieces(sums), w_ref[...])
    sets = sums.shape[0]
    average = (three[:sets] + (three[sets : 2 * sets] + three[2 * sets :])) / rows
    spread = squares / rows - average * average
    scale = lax.rsqrt(spread + EPS) * gain_ref[...]
    scale_s[...] = reorder(by_image, scale)
    shift_s[...] = reorder(by_image, shift_ref[...] - average * scale)
    for j in range(0, wide, COLUMNS):
        cols = slice(j, j + COLUMNS)
        sc, sh = scale_s[:, cols], shift_s[:, cols]
        total = jnp.zeros((count, COLUMNS), F32)
        for place in range(places):
            y = e_ref[place, :, cols] * sc + sh + x_ref[place, :, cols].astype(F32)
            total += jnp.maximum(y, 0.0)
        pool[:, cols] = total
    pooled = (pool[...] / places).astype(BF16)
    u = dot32(pooled, proj_ref[...])
    key = (u * lax.rsqrt(jnp.sum(u * u, 1, keepdims=True) + UNIT_EPS)).astype(BF16)
    key_ref[...] = key
    copies_ref[...] = jnp.broadcast_to(key[None], copies_ref.shape)


def merge_stage(rows, core, peers, e, x, mine, other, by_image, gain, shift, weight, proj):
    places, count, wide = e.shape
    feat = proj.shape[1]
    return pl.pallas_call(
        functools.partial(merge_kernel, rows),
        name="merge",
        in_specs=[SMEM] + [VMEM] * 9,
        out_specs=[VMEM] * 2,
        out_shape=[
            jax.ShapeDtypeStruct((count, feat), BF16),
            jax.ShapeDtypeStruct((peers, count, feat), BF16),
        ],
        scratch_shapes=[
            pltpu.VMEM((count, wide), F32),
            pltpu.VMEM((count, wide), F32),
            pltpu.VMEM((count, wide), F32),
        ],
        compiler_params=pltpu.CompilerParams(vmem_limit_bytes=16 * 1024 * 1024),
        cost_estimate=pl.CostEstimate(
            flops=8 * places * count * wide,
            bytes_accessed=2 * x.size + 4 * e.size,
            transcendentals=0,
        ),
    )(core, e, x, mine, other, by_image, gain, shift, weight, proj)


def negative_kernel(factor, q_ref, k_ref, out_ref):
    @pl.when(pl.program_id(0) == 0)
    def _():
        out_ref[...] = jnp.zeros_like(out_ref)

    keys = k_ref[...]
    wide = keys.astype(F32)
    norm = lax.rsqrt(jnp.sum(wide * wide, 1, keepdims=True) + UNIT_EPS) * factor
    score = lax.dot_general(
        keys, q_ref[...], (((1,), (1,)), ((), ())), preferred_element_type=F32
    )
    out_ref[...] += jnp.sum(jnp.exp2(score * norm), 0, keepdims=True)


def negative_stage(queries, keys, part, parts):
    count, feat = queries.shape
    total = keys.shape[0] // parts
    block = math.gcd(total, 2048)
    steps = total // block
    return pl.pallas_call(
        functools.partial(negative_kernel, math.log2(math.e) / TEMP),
        name="negative",
        grid=(steps,),
        in_specs=[VMEM, pl.BlockSpec((block, feat), lambda i: (i + part * steps, 0))],
        out_specs=pl.BlockSpec((1, count), lambda i: (0, 0)),
        out_shape=jax.ShapeDtypeStruct((1, count), F32),
        compiler_params=params(8),
        cost_estimate=pl.CostEstimate(
            flops=2 * total * count * feat,
            bytes_accessed=2 * total * feat,
            transcendentals=total * count,
        ),
    )(queries, keys)


def loss_kernel(table_ref, u_ref, pos_ref, neg_ref, loss_ref):
    logits = lax.dot_general(
        table_ref[...], u_ref[...], (((1,), (1,)), ((), ())), preferred_element_type=F32
    )
    row = lax.broadcasted_iota(jnp.int32, logits.shape, 0)
    picked = jnp.sum(jnp.where(row == pos_ref[...], logits, 0.0), 0, keepdims=True) / TEMP
    loss_ref[...] = jnp.log(jnp.exp(picked) + neg_ref[...]) - picked


def loss_stage(table, units, positive, negatives):
    return pl.pallas_call(
        loss_kernel,
        name="loss",
        in_specs=[VMEM] * 4,
        out_specs=VMEM,
        out_shape=jax.ShapeDtypeStruct(positive.shape, F32),
        compiler_params=pltpu.CompilerParams(vmem_limit_bytes=8 * 1024 * 1024),
    )(table, units, positive, negatives)


def unit_rows(values):
    as_float = values.astype(F32)
    return (
        as_float * lax.rsqrt(jnp.sum(as_float * as_float, -1, keepdims=True) + UNIT_EPS)
    ).astype(BF16)


RING = 4


def swap_core():
    return [(i, i ^ 1) for i in range(2 * RING * RING)]


def ring_swap(k, flip):
    pairs = []
    for i in range(2 * RING * RING):
        x, z, c = i // (2 * RING), (i // 2) % RING, i % 2
        if (c == 1) != flip:
            x = x ^ k
        else:
            z = z ^ k
        pairs.append((i, (x * RING + z) * 2 + c))
    return pairs


def queue_swap(values, k):
    return lax.ppermute(values, "queue", [(i, i ^ k) for i in range(RING)])


def reduce_sets(keep, send, side_work, side_input):
    total = keep + lax.ppermute(send, "dp", swap_core())
    for flip, work in zip((False, True), side_work):
        parts = [lax.ppermute(total, "dp", ring_swap(k, flip)) for k in (1, 2, 3)]
        side_input, _ = lax.optimization_barrier((side_input, total))
        side_input = work(side_input)
        parts, side_input = lax.optimization_barrier((parts, side_input))
        total = (total + parts[0]) + (parts[1] + parts[2])
    return total, lax.ppermute(total, "dp", swap_core()), side_input


def on_device(
    features,
    shuffle,
    positive,
    queries,
    queue_keys,
    reduce_weight,
    gain_one,
    shift_one,
    w_spatial,
    gain_two,
    shift_two,
    w_expand,
    gain_three,
    shift_three,
    w_project,
):
    count, places, channels = features.shape
    peers = lax.axis_size("dp")
    me = lax.axis_index("dp").astype(jnp.int32).reshape(1)
    core = jnp.bitwise_and(me, 1)
    rows = count * places
    x = jnp.transpose(features, (1, 0, 2))
    units = unit_rows(queries)

    first = queue_swap(units, 1)

    def gather(pair):
        return jnp.concatenate([pair, queue_swap(pair, 3)], 0)

    def negative_one(queries_here):
        return queries_here, negative_stage(queries_here, queue_keys, 0, 2)

    def negative_two(state):
        return state[1] + negative_stage(state[0], queue_keys, 1, 2)

    def return_one(sums):
        return sums[:, : 2 * count] + queue_swap(sums[:, 2 * count :], 3)

    def return_two(sums):
        return sums[:, :count] + queue_swap(sums[:, count:], 1)

    y, keep, send, by_set, by_image, x = reduce_stage(me, x, reduce_weight, shuffle)
    pair = jnp.concatenate([units, first], 0)
    mine, other, state = reduce_sets(keep, send, (gather, negative_one), pair)
    z, keep, send = conv_stage(
        rows, core, y, mine, other, by_set, by_image, gain_one[None], shift_one[None], w_spatial
    )
    mine, other, sums = reduce_sets(keep, send, (negative_two, return_one), state)
    e, keep, send = expand_stage(
        rows, core, z, mine, other, by_set, by_image, gain_two[None], shift_two[None], w_expand
    )
    mine, other, negatives = reduce_sets(keep, send, (return_two, lambda v: v), sums)
    key_rows, copies = merge_stage(
        rows,
        core,
        peers,
        e,
        x,
        mine,
        other,
        by_image,
        gain_three[None],
        shift_three[None],
        w_expand,
        w_project,
    )
    table = lax.all_to_all(copies, "dp", split_axis=0, concat_axis=0, tiled=True)
    table = table.reshape(peers * count, -1)
    loss_vals = loss_stage(table, units, positive.reshape(1, count), negatives)
    return (loss_vals.reshape(count), key_rows)


def solution(mesh):
    placed = (
        P(("queue", "dp"), None, None),
        P("queue", None),
        P(("queue", "dp")),
        P(("queue", "dp"), None),
        P("queue", None),
    ) + (P(),) * 10
    return jax.shard_map(
        on_device,
        mesh=mesh,
        in_specs=placed,
        out_specs=(P(("queue", "dp")), P(("queue", "dp"), None)),
        check_vma=False,
    )
```

```python
import functools
import math

import jax
import jax.numpy as jnp
from jax import lax
from jax.experimental import pallas as pl
from jax.experimental.pallas import tpu as pltpu
from jax.sharding import PartitionSpec as P


SIDE = 7
EPS = 1e-05
UNIT_EPS = 1e-06
TEMP = 0.2
F32 = jnp.float32
BF16 = jnp.bfloat16
VMEM = pl.BlockSpec(memory_space=pltpu.VMEM)
SMEM = pl.BlockSpec(memory_space=pltpu.SMEM)


def params(limit_mib):
    return pltpu.CompilerParams(
        dimension_semantics=("arbitrary",), vmem_limit_bytes=limit_mib * 1024 * 1024
    )


def dot32(a, b):
    return jnp.dot(a, b, preferred_element_type=F32)


def pieces(values):
    high = values.astype(BF16)
    rest = values - high.astype(F32)
    middle = rest.astype(BF16)
    low = (rest - middle.astype(F32)).astype(BF16)
    return jnp.concatenate([high, middle, low], 0)


def set_onehots(me, shuffle, count):
    total = shuffle.shape[1]
    image = lax.broadcasted_iota(jnp.int32, (count, total), 0) + me * count
    here = (shuffle == image).astype(F32)
    slot = lax.broadcasted_iota(jnp.int32, (total, total // count), 0)
    low = lax.broadcasted_iota(jnp.int32, (total, total // count), 1) * count
    inside = jnp.logical_and(slot >= low, slot < low + count)
    by_image = dot32(here.astype(BF16), inside.astype(F32).astype(BF16))
    by_set = jnp.transpose(by_image, (1, 0))
    return [jnp.concatenate([p] * 3, 1).astype(BF16) for p in (by_set, by_image)]


def reorder(onehot, values):
    return dot32(onehot, pieces(values))


def split_halves(core, values, keep_ref, send_ref, start):
    half = values.shape[1] // 2
    low, high = values[:, :half], values[:, half:]
    keep_ref[:, start : start + half] = jnp.where(core == 0, low, high)
    send_ref[:, start : start + half] = jnp.where(core == 0, high, low)


def join_halves(core, mine, other):
    low = jnp.where(core == 0, mine, other)
    high = jnp.where(core == 0, other, mine)
    return jnp.concatenate([low, high], 1)


CHUNKS = ((0, 7), (7, 14), (21, 28))


def reduce_kernel(
    me_ref,
    x_hbm,
    w_hbm,
    shuffle_hbm,
    y_ref,
    keep_ref,
    send_ref,
    by_set_ref,
    by_image_ref,
    x_ref,
    w_ref,
    shuffle_ref,
    sems,
):
    _, count, channels = x_ref.shape
    mid = w_ref.shape[1]
    weight_copy = pltpu.make_async_copy(w_hbm, w_ref, sems.at[0])
    weight_copy.start()
    copies = []
    for n, (first, size) in enumerate(CHUNKS):
        part = pl.ds(first, size)
        copies.append(pltpu.make_async_copy(x_hbm.at[part], x_ref.at[part], sems.at[n + 1]))
        copies[-1].start()
    shuffle_copy = pltpu.make_async_copy(shuffle_hbm, shuffle_ref, sems.at[len(CHUNKS) + 1])
    shuffle_copy.start()
    shuffle_copy.wait()
    by_set, by_image = set_onehots(me_ref[0], shuffle_ref[...], count)
    by_set_ref[...] = by_set
    by_image_ref[...] = by_image
    weight_copy.wait()
    s1 = jnp.zeros((count, mid), F32)
    s2 = jnp.zeros((count, mid), F32)
    for (first, size), copy in zip(CHUNKS, copies):
        copy.wait()
        part = pl.ds(first, size)
        y = dot32(x_ref[part].reshape(size * count, channels), w_ref[...])
        y = y.reshape(size, count, mid)
        y_ref[part] = y
        s1 += jnp.sum(y, 0)
        s2 += jnp.sum(y * y, 0)
    core = jnp.bitwise_and(me_ref[0], 1)
    split_halves(core, reorder(by_set, s1), keep_ref, send_ref, 0)
    split_halves(core, reorder(by_set, s2), keep_ref, send_ref, mid // 2)


def reduce_stage(me, x, weight, shuffle):
    places, count, channels = x.shape
    mid = weight.shape[1]
    sets = shuffle.shape[1] // count
    hbm = pl.BlockSpec(memory_space=pltpu.HBM)
    return pl.pallas_call(
        reduce_kernel,
        name="reduce",
        in_specs=[SMEM, hbm, hbm, hbm],
        out_specs=[VMEM] * 6,
        out_shape=[
            jax.ShapeDtypeStruct((places, count, mid), F32),
            jax.ShapeDtypeStruct((count, mid), F32),
            jax.ShapeDtypeStruct((count, mid), F32),
            jax.ShapeDtypeStruct((sets, 3 * count), BF16),
            jax.ShapeDtypeStruct((count, 3 * sets), BF16),
            jax.ShapeDtypeStruct(x.shape, x.dtype),
        ],
        scratch_shapes=[
            pltpu.VMEM(weight.shape, weight.dtype),
            pltpu.VMEM(shuffle.shape, shuffle.dtype),
            pltpu.SemaphoreType.DMA((len(CHUNKS) + 2,)),
        ],
        compiler_params=pltpu.CompilerParams(vmem_limit_bytes=24 * 1024 * 1024),
        cost_estimate=pl.CostEstimate(
            flops=2 * places * count * channels * mid,
            bytes_accessed=2 * x.size + 4 * places * count * mid,
            transcendentals=0,
        ),
    )(me, *[pltpu.with_memory_space_constraint(v, pltpu.HBM) for v in (x, weight, shuffle)])


def scale_shift(core, mine, other, onehot, gain, shift, rows):
    half = mine.shape[1] // 2
    total1 = join_halves(core, mine[:, :half], other[:, :half])
    total2 = join_halves(core, mine[:, half:], other[:, half:])
    average = total1 / rows
    spread = total2 / rows - average * average
    scale = lax.rsqrt(spread + EPS) * gain
    return reorder(onehot, scale), reorder(onehot, shift - average * scale)


def conv_kernel(
    rows,
    core_ref,
    y_ref,
    mine_ref,
    other_ref,
    by_set_ref,
    by_image_ref,
    gain_ref,
    shift_ref,
    w_ref,
    z_ref,
    keep_ref,
    send_ref,
    act,
    scale_s,
    shift_s,
    s1,
    s2,
):
    step = pl.program_id(0)
    side = SIDE
    _, count, mid = y_ref.shape

    def norm(row):
        a = y_ref[pl.ds(row * side, side)] * scale_s[...][None] + shift_s[...][None]
        act[row] = jnp.maximum(a, 0.0).astype(BF16)

    def conv_row(row, dys):
        for dx in (0, -1, 1):
            lo, hi = max(0, -dx), side - max(0, dx)
            window = [act[row + dy, lo + dx : hi + dx].reshape((hi - lo) * count, mid) for dy in dys]
            weight = [w_ref[3 * (dy + 1) + dx + 1] for dy in dys]
            part = dot32(jnp.concatenate(window, 1), jnp.concatenate(weight, 0))
            part = part.reshape(hi - lo, count, mid)
            if dx == 0:
                z_ref[pl.ds(row * side, side)] = part
            else:
                z_ref[pl.ds(row * side + lo, hi - lo)] += part
        z = z_ref[pl.ds(row * side, side)]
        s1[...] += jnp.sum(z, 0)
        s2[...] += jnp.sum(z * z, 0)

    @pl.when(step == 0)
    def _():
        scale, shift = scale_shift(
            core_ref[0],
            mine_ref[...],
            other_ref[...],
            by_image_ref[...],
            gain_ref[...],
            shift_ref[...],
            rows,
        )
        scale_s[...] = scale
        shift_s[...] = shift
        s1[...] = jnp.zeros_like(s1)
        s2[...] = jnp.zeros_like(s2)
        norm(0)
        norm(1)
        conv_row(0, (0, 1))
        norm(2)

    @pl.when(jnp.logical_and(step > 0, step < side - 1))
    def _():
        conv_row(step, (-1, 0, 1))
        norm(jnp.minimum(step + 2, side - 1))

    @pl.when(step == side - 1)
    def _():
        conv_row(side - 1, (-1, 0))
        core = core_ref[0]
        by_set = by_set_ref[...]
        split_halves(core, reorder(by_set, s1[...]), keep_ref, send_ref, 0)
        split_halves(core, reorder(by_set, s2[...]), keep_ref, send_ref, mid // 2)


def conv_stage(rows, core, y, mine, other, by_set, by_image, gain, shift, weight):
    places, count, mid = y.shape
    return pl.pallas_call(
        functools.partial(conv_kernel, rows),
        name="conv",
        grid=(SIDE,),
        in_specs=[SMEM] + [VMEM] * 8,
        out_specs=[VMEM] * 3,
        out_shape=[
            jax.ShapeDtypeStruct((places, count, mid), F32),
            jax.ShapeDtypeStruct((count, mid), F32),
            jax.ShapeDtypeStruct((count, mid), F32),
        ],
        scratch_shapes=[
            pltpu.VMEM((SIDE, SIDE, count, mid), BF16),
            pltpu.VMEM((count, mid), F32),
            pltpu.VMEM((count, mid), F32),
            pltpu.VMEM((count, mid), F32),
            pltpu.VMEM((count, mid), F32),
        ],
        compiler_params=params(16),
        cost_estimate=pl.CostEstimate(
            flops=2 * 361 * count * mid * mid,
            bytes_accessed=8 * places * count * mid + 2 * weight.size,
            transcendentals=0,
        ),
    )(core, y, mine, other, by_set, by_image, gain, shift, weight)


COLUMNS = 256


def center_kernel(gain_ref, shift_ref, w_ref, act_center_ref, center_ref):
    gain, shift = gain_ref[...], shift_ref[...]
    ratio = jnp.abs(shift) / gain
    value = jnp.maximum(shift, 0.0) + 0.4 * gain * jnp.exp(-ratio * (1.1 + 0.45 * ratio))
    value = value.astype(BF16)
    act_center_ref[...] = value.astype(F32)
    wide = dot32(jnp.broadcast_to(value, (16, value.shape[1])), w_ref[...])
    center_ref[...] = wide[:1]


def center_stage(gain, shift, weight):
    return pl.pallas_call(
        center_kernel,
        name="center",
        in_specs=[VMEM] * 3,
        out_specs=[VMEM] * 2,
        out_shape=[
            jax.ShapeDtypeStruct(gain.shape, F32),
            jax.ShapeDtypeStruct((1, weight.shape[1]), F32),
        ],
        compiler_params=pltpu.CompilerParams(vmem_limit_bytes=8 * 1024 * 1024),
        cost_estimate=pl.CostEstimate(
            flops=32 * weight.size, bytes_accessed=2 * weight.size, transcendentals=gain.size
        ),
    )(gain, shift, weight)


def expand_kernel(
    rows,
    core_ref,
    z_ref,
    mine_ref,
    other_ref,
    by_set_ref,
    by_image_ref,
    gain_ref,
    shift_ref,
    act_center_ref,
    center_ref,
    w_ref,
    e_ref,
    keep_ref,
    send_ref,
    act,
    sq_s,
):
    places, count, mid = z_ref.shape
    wide = w_ref.shape[1]
    core = core_ref[0]
    by_set = by_set_ref[...]
    scale, shift = scale_shift(
        core,
        mine_ref[...],
        other_ref[...],
        by_image_ref[...],
        gain_ref[...],
        shift_ref[...],
        rows,
    )
    total = jnp.zeros((count, mid), F32)
    for row in range(0, places, SIDE):
        a = z_ref[row : row + SIDE] * scale[None] + shift[None]
        a = jnp.maximum(a, 0.0).astype(BF16)
        act[row : row + SIDE] = a
        total += jnp.sum(a.astype(F32), 0)
    flat = act[...].reshape(places * count, mid)
    for j in range(0, wide, COLUMNS):
        e = dot32(flat, w_ref[:, j : j + COLUMNS]).reshape(places, count, COLUMNS)
        e_ref[:, :, j : j + COLUMNS] = e
        d = e - center_ref[:, j : j + COLUMNS][None]
        sq_s[:, j : j + COLUMNS] = jnp.sum(d * d, 0)
    total = total - places * act_center_ref[...]
    split_halves(core, reorder(by_set, total), keep_ref, send_ref, 0)
    split_halves(core, reorder(by_set, sq_s[...]), keep_ref, send_ref, mid // 2)


def expand_stage(
    rows, core, z, mine, other, by_set, by_image, gain, shift, act_center, center, weight
):
    places, count, mid = z.shape
    wide = weight.shape[1]
    sums = (mid + wide) // 2
    return pl.pallas_call(
        functools.partial(expand_kernel, rows),
        name="expand",
        in_specs=[SMEM] + [VMEM] * 10,
        out_specs=[VMEM] * 3,
        out_shape=[
            jax.ShapeDtypeStruct((places, count, wide), F32),
            jax.ShapeDtypeStruct((count, sums), F32),
            jax.ShapeDtypeStruct((count, sums), F32),
        ],
        scratch_shapes=[
            pltpu.VMEM((places, count, mid), BF16),
            pltpu.VMEM((count, wide), F32),
        ],
        compiler_params=pltpu.CompilerParams(vmem_limit_bytes=16 * 1024 * 1024),
        cost_estimate=pl.CostEstimate(
            flops=2 * places * count * mid * wide,
            bytes_accessed=4 * places * count * (mid + wide),
            transcendentals=0,
        ),
    )(core, z, mine, other, by_set, by_image, gain, shift, act_center, center, weight)


def merge_kernel(
    rows,
    core_ref,
    e_ref,
    x_ref,
    mine_ref,
    other_ref,
    by_image_ref,
    gain_ref,
    shift_ref,
    act_center_ref,
    center_ref,
    w_ref,
    proj_ref,
    key_ref,
    copies_ref,
    scale_s,
    shift_s,
    pool,
):
    places, count, wide = e_ref.shape
    core, by_image = core_ref[0], by_image_ref[...]
    mine, other = mine_ref[...], other_ref[...]
    cut = w_ref.shape[0] // 2
    sums = join_halves(core, mine[:, :cut], other[:, :cut]) + rows * act_center_ref[...]
    squares = join_halves(core, mine[:, cut:], other[:, cut:])
    three = dot32(pieces(sums), w_ref[...])
    sets = sums.shape[0]
    average = (three[:sets] + (three[sets : 2 * sets] + three[2 * sets :])) / rows
    away = average - center_ref[...]
    spread = squares / rows - away * away
    scale = lax.rsqrt(spread + EPS) * gain_ref[...]
    scale_s[...] = reorder(by_image, scale)
    shift_s[...] = reorder(by_image, shift_ref[...] - average * scale)
    for j in range(0, wide, COLUMNS):
        cols = slice(j, j + COLUMNS)
        sc, sh = scale_s[:, cols], shift_s[:, cols]
        total = jnp.zeros((count, COLUMNS), F32)
        for place in range(places):
            y = e_ref[place, :, cols] * sc + sh + x_ref[place, :, cols].astype(F32)
            total += jnp.maximum(y, 0.0)
        pool[:, cols] = total
    pooled = (pool[...] / places).astype(BF16)
    u = dot32(pooled, proj_ref[...])
    key = (u * lax.rsqrt(jnp.sum(u * u, 1, keepdims=True) + UNIT_EPS)).astype(BF16)
    key_ref[...] = key
    copies_ref[...] = jnp.broadcast_to(key[None], copies_ref.shape)


def merge_stage(
    rows, core, peers, e, x, mine, other, by_image, gain, shift, act_center, center, weight, proj
):
    places, count, wide = e.shape
    feat = proj.shape[1]
    return pl.pallas_call(
        functools.partial(merge_kernel, rows),
        name="merge",
        in_specs=[SMEM] + [VMEM] * 11,
        out_specs=[VMEM] * 2,
        out_shape=[
            jax.ShapeDtypeStruct((count, feat), BF16),
            jax.ShapeDtypeStruct((peers, count, feat), BF16),
        ],
        scratch_shapes=[
            pltpu.VMEM((count, wide), F32),
            pltpu.VMEM((count, wide), F32),
            pltpu.VMEM((count, wide), F32),
        ],
        compiler_params=pltpu.CompilerParams(vmem_limit_bytes=16 * 1024 * 1024),
        cost_estimate=pl.CostEstimate(
            flops=8 * places * count * wide,
            bytes_accessed=2 * x.size + 4 * e.size,
            transcendentals=0,
        ),
    )(core, e, x, mine, other, by_image, gain, shift, act_center, center, weight, proj)


def negative_kernel(factor, q_ref, k_ref, out_ref):
    @pl.when(pl.program_id(0) == 0)
    def _():
        out_ref[...] = jnp.zeros_like(out_ref)

    keys = k_ref[...]
    wide = keys.astype(F32)
    norm = lax.rsqrt(jnp.sum(wide * wide, 1, keepdims=True) + UNIT_EPS) * factor
    score = lax.dot_general(
        keys, q_ref[...], (((1,), (1,)), ((), ())), preferred_element_type=F32
    )
    out_ref[...] += jnp.sum(jnp.exp2(score * norm), 0, keepdims=True)


def negative_stage(queries, keys, part, parts):
    count, feat = queries.shape
    total = keys.shape[0] // parts
    block = math.gcd(total, 2048)
    steps = total // block
    return pl.pallas_call(
        functools.partial(negative_kernel, math.log2(math.e) / TEMP),
        name="negative",
        grid=(steps,),
        in_specs=[VMEM, pl.BlockSpec((block, feat), lambda i: (i + part * steps, 0))],
        out_specs=pl.BlockSpec((1, count), lambda i: (0, 0)),
        out_shape=jax.ShapeDtypeStruct((1, count), F32),
        compiler_params=params(8),
        cost_estimate=pl.CostEstimate(
            flops=2 * total * count * feat,
            bytes_accessed=2 * total * feat,
            transcendentals=total * count,
        ),
    )(queries, pltpu.with_memory_space_constraint(keys, pltpu.HBM))


def loss_kernel(table_ref, u_ref, pos_ref, neg_ref, loss_ref):
    logits = lax.dot_general(
        table_ref[...], u_ref[...], (((1,), (1,)), ((), ())), preferred_element_type=F32
    )
    row = lax.broadcasted_iota(jnp.int32, logits.shape, 0)
    picked = jnp.sum(jnp.where(row == pos_ref[...], logits, 0.0), 0, keepdims=True) / TEMP
    loss_ref[...] = jnp.log(jnp.exp(picked) + neg_ref[...]) - picked


def loss_stage(table, units, positive, negatives):
    return pl.pallas_call(
        loss_kernel,
        name="loss",
        in_specs=[VMEM] * 4,
        out_specs=VMEM,
        out_shape=jax.ShapeDtypeStruct(positive.shape, F32),
        compiler_params=pltpu.CompilerParams(vmem_limit_bytes=8 * 1024 * 1024),
    )(table, units, positive, negatives)


def unit_rows(values):
    as_float = values.astype(F32)
    return (
        as_float * lax.rsqrt(jnp.sum(as_float * as_float, -1, keepdims=True) + UNIT_EPS)
    ).astype(BF16)


RING = 4


def swap_core():
    return [(i, i ^ 1) for i in range(2 * RING * RING)]


def ring_swap(k, flip):
    pairs = []
    for i in range(2 * RING * RING):
        x, z, c = i // (2 * RING), (i // 2) % RING, i % 2
        if (c == 1) != flip:
            x = x ^ k
        else:
            z = z ^ k
        pairs.append((i, (x * RING + z) * 2 + c))
    return pairs


def queue_swap(values, k):
    return lax.ppermute(values, "queue", [(i, i ^ k) for i in range(RING)])


def reduce_sets(keep, send, side_work, side_input, wire):
    total = keep + lax.ppermute(send, "dp", swap_core())
    for turn, work in enumerate(side_work):
        parts = []
        sent = total.astype(wire)
        for k in (1, 2, 3):
            parts.append(lax.ppermute(sent, "dp", ring_swap(k, turn == 1)).astype(F32))
        held, free = work(lax.optimization_barrier((side_input, total))[0])
        parts, held = lax.optimization_barrier((parts, held))
        side_input = (held, free)
        total = (total + parts[0]) + (parts[1] + parts[2])
    return total, lax.ppermute(total, "dp", swap_core()), side_input


def on_device(
    features,
    shuffle,
    positive,
    queries,
    queue_keys,
    reduce_weight,
    gain_one,
    shift_one,
    w_spatial,
    gain_two,
    shift_two,
    w_expand,
    gain_three,
    shift_three,
    w_project,
):
    count, places, _ = features.shape
    peers = lax.axis_size("dp")
    me = lax.axis_index("dp").astype(jnp.int32).reshape(1)
    core = jnp.bitwise_and(me, 1)
    rows = count * places
    x = jnp.transpose(features, (1, 0, 2))
    units = unit_rows(queries)
    gain_two, shift_two = gain_two[None], shift_two[None]

    def gather_one(own):
        return None, (own, queue_swap(own, 1))

    def gather_two(state):
        pair = jnp.concatenate(state[1], 0)
        return None, (pair, queue_swap(pair, 3))

    def negative_one(state):
        here, gain, shift = state
        centers = center_stage(gain, shift, w_expand)
        return (here, negative_stage(here, queue_keys, 0, 2), centers), None

    def negative_two(state):
        here, sums, centers = state[0]
        sums = sums + negative_stage(here, queue_keys, 1, 2)
        return (sums, centers), queue_swap(sums[:, 2 * count :], 3)

    def return_two(state):
        sums = state[0] + state[1]
        return None, (sums[:, :count], queue_swap(sums[:, count:], 1))

    def return_done(state):
        return sum(state[1]), None

    y, keep, send, by_set, by_image, x = reduce_stage(me, x, reduce_weight, shuffle)
    mine, other, (_, asked) = reduce_sets(keep, send, (gather_one, gather_two), units, F32)
    asked = jnp.concatenate(asked, 0)
    z, keep, send = conv_stage(
        rows, core, y, mine, other, by_set, by_image, gain_one[None], shift_one[None], w_spatial
    )
    mine, other, ((sums, centers), told) = reduce_sets(
        keep, send, (negative_one, negative_two), (asked, gain_two, shift_two), F32
    )
    e, keep, send = expand_stage(
        rows, core, z, mine, other, by_set, by_image, gain_two, shift_two, *centers, w_expand
    )
    mine, other, (negatives, _) = reduce_sets(
        keep, send, (return_two, return_done), (sums[:, : 2 * count], told), BF16
    )
    key_rows, copies = merge_stage(
        rows,
        core,
        peers,
        e,
        x,
        mine,
        other,
        by_image,
        gain_three[None],
        shift_three[None],
        *centers,
        w_expand,
        w_project,
    )
    table = lax.all_to_all(copies, "dp", split_axis=0, concat_axis=0, tiled=True)
    table = table.reshape(peers * count, -1)
    loss_vals = loss_stage(table, units, positive.reshape(1, count), negatives)
    return (loss_vals.reshape(count), key_rows)


def solution(mesh):
    placed = (
        P(("queue", "dp"), None, None),
        P("queue", None),
        P(("queue", "dp")),
        P(("queue", "dp"), None),
        P("queue", None),
    ) + (P(),) * 10
    return jax.shard_map(
        on_device,
        mesh=mesh,
        in_specs=placed,
        out_specs=(P(("queue", "dp")), P(("queue", "dp"), None)),
        check_vma=False,
    )
```

```python
import functools
import math

import jax
import jax.numpy as jnp
from jax import lax
from jax.experimental import pallas as pl
from jax.experimental.pallas import tpu as pltpu
from jax.sharding import PartitionSpec as P


SIDE = 7
EPS = 1e-05
UNIT_EPS = 1e-06
TEMP = 0.2
F32 = jnp.float32
BF16 = jnp.bfloat16
VMEM = pl.BlockSpec(memory_space=pltpu.VMEM)
SMEM = pl.BlockSpec(memory_space=pltpu.SMEM)


def params(limit_mib):
    return pltpu.CompilerParams(
        dimension_semantics=("arbitrary",), vmem_limit_bytes=limit_mib * 1024 * 1024
    )


def dot32(a, b):
    return jnp.dot(a, b, preferred_element_type=F32)


def pieces(values):
    high = values.astype(BF16)
    rest = values - high.astype(F32)
    middle = rest.astype(BF16)
    low = (rest - middle.astype(F32)).astype(BF16)
    return jnp.concatenate([high, middle, low], 0)


def set_onehots(me, shuffle, count):
    total = shuffle.shape[1]
    image = lax.broadcasted_iota(jnp.int32, (count, total), 0) + me * count
    here = (shuffle == image).astype(F32)
    slot = lax.broadcasted_iota(jnp.int32, (total, total // count), 0)
    low = lax.broadcasted_iota(jnp.int32, (total, total // count), 1) * count
    inside = jnp.logical_and(slot >= low, slot < low + count)
    by_image = dot32(here.astype(BF16), inside.astype(F32).astype(BF16))
    by_set = jnp.transpose(by_image, (1, 0))
    return [jnp.concatenate([p] * 3, 1).astype(BF16) for p in (by_set, by_image)]


def reorder(onehot, values):
    return dot32(onehot, pieces(values))


def split_halves(core, values, keep_ref, send_ref, start):
    half = values.shape[1] // 2
    low, high = values[:, :half], values[:, half:]
    keep_ref[:, start : start + half] = jnp.where(core == 0, low, high)
    send_ref[:, start : start + half] = jnp.where(core == 0, high, low)


def join_halves(core, mine, other):
    low = jnp.where(core == 0, mine, other)
    high = jnp.where(core == 0, other, mine)
    return jnp.concatenate([low, high], 1)


CHUNKS = ((0, 7), (7, 14), (21, 28))


def reduce_kernel(
    me_ref,
    x_hbm,
    w_hbm,
    shuffle_hbm,
    y_ref,
    keep_ref,
    send_ref,
    by_set_ref,
    by_image_ref,
    x_ref,
    w_ref,
    shuffle_ref,
    sems,
):
    _, count, channels = x_ref.shape
    mid = w_ref.shape[1]
    shuffle_copy = pltpu.make_async_copy(shuffle_hbm, shuffle_ref, sems.at[len(CHUNKS) + 1])
    shuffle_copy.start()
    weight_copy = pltpu.make_async_copy(w_hbm, w_ref, sems.at[0])
    weight_copy.start()
    copies = []
    for n, (first, size) in enumerate(CHUNKS):
        part = pl.ds(first, size)
        copies.append(pltpu.make_async_copy(x_hbm.at[part], x_ref.at[part], sems.at[n + 1]))
        copies[-1].start()
    shuffle_copy.wait()
    by_set, by_image = set_onehots(me_ref[0], shuffle_ref[...], count)
    by_set_ref[...] = by_set
    by_image_ref[...] = by_image
    weight_copy.wait()
    s1 = jnp.zeros((count, mid), F32)
    s2 = jnp.zeros((count, mid), F32)
    for (first, size), copy in zip(CHUNKS, copies):
        copy.wait()
        part = pl.ds(first, size)
        y = dot32(x_ref[part].reshape(size * count, channels), w_ref[...])
        y = y.reshape(size, count, mid)
        y_ref[part] = y
        s1 += jnp.sum(y, 0)
        s2 += jnp.sum(y * y, 0)
    core = jnp.bitwise_and(me_ref[0], 1)
    split_halves(core, reorder(by_set, s1), keep_ref, send_ref, 0)
    split_halves(core, reorder(by_set, s2), keep_ref, send_ref, mid // 2)


def reduce_stage(me, x, weight, shuffle):
    places, count, channels = x.shape
    mid = weight.shape[1]
    sets = shuffle.shape[1] // count
    hbm = pl.BlockSpec(memory_space=pltpu.HBM)
    return pl.pallas_call(
        reduce_kernel,
        name="reduce",
        in_specs=[SMEM, hbm, hbm, hbm],
        out_specs=[VMEM] * 6,
        out_shape=[
            jax.ShapeDtypeStruct((places, count, mid), F32),
            jax.ShapeDtypeStruct((count, mid), F32),
            jax.ShapeDtypeStruct((count, mid), F32),
            jax.ShapeDtypeStruct((sets, 3 * count), BF16),
            jax.ShapeDtypeStruct((count, 3 * sets), BF16),
            jax.ShapeDtypeStruct(x.shape, x.dtype),
        ],
        scratch_shapes=[
            pltpu.VMEM(weight.shape, weight.dtype),
            pltpu.VMEM(shuffle.shape, shuffle.dtype),
            pltpu.SemaphoreType.DMA((len(CHUNKS) + 2,)),
        ],
        compiler_params=pltpu.CompilerParams(vmem_limit_bytes=24 * 1024 * 1024),
        cost_estimate=pl.CostEstimate(
            flops=2 * places * count * channels * mid,
            bytes_accessed=2 * x.size + 4 * places * count * mid,
            transcendentals=0,
        ),
    )(me, *[pltpu.with_memory_space_constraint(v, pltpu.HBM) for v in (x, weight, shuffle)])


def scale_shift(core, mine, other, onehot, gain, shift, rows):
    half = mine.shape[1] // 2
    total1 = join_halves(core, mine[:, :half], other[:, :half])
    total2 = join_halves(core, mine[:, half:], other[:, half:])
    average = total1 / rows
    spread = total2 / rows - average * average
    scale = lax.rsqrt(spread + EPS) * gain
    return reorder(onehot, scale), reorder(onehot, shift - average * scale)


def conv_kernel(
    rows,
    core_ref,
    y_ref,
    mine_ref,
    other_ref,
    by_set_ref,
    by_image_ref,
    gain_ref,
    shift_ref,
    w_ref,
    z_ref,
    keep_ref,
    send_ref,
    act,
    scale_s,
    shift_s,
    s1,
    s2,
):
    step = pl.program_id(0)
    side = SIDE
    _, count, mid = y_ref.shape

    def norm(row):
        a = y_ref[pl.ds(row * side, side)] * scale_s[...][None] + shift_s[...][None]
        act[row] = jnp.maximum(a, 0.0).astype(BF16)

    def conv_row(row, dys):
        for dx in (0, -1, 1):
            lo, hi = max(0, -dx), side - max(0, dx)
            window = [act[row + dy, lo + dx : hi + dx].reshape((hi - lo) * count, mid) for dy in dys]
            weight = [w_ref[3 * (dy + 1) + dx + 1] for dy in dys]
            part = dot32(jnp.concatenate(window, 1), jnp.concatenate(weight, 0))
            part = part.reshape(hi - lo, count, mid)
            if dx == 0:
                z_ref[pl.ds(row * side, side)] = part
            else:
                z_ref[pl.ds(row * side + lo, hi - lo)] += part
        z = z_ref[pl.ds(row * side, side)]
        s1[...] += jnp.sum(z, 0)
        s2[...] += jnp.sum(z * z, 0)

    @pl.when(step == 0)
    def _():
        scale, shift = scale_shift(
            core_ref[0],
            mine_ref[...],
            other_ref[...],
            by_image_ref[...],
            gain_ref[...],
            shift_ref[...],
            rows,
        )
        scale_s[...] = scale
        shift_s[...] = shift
        s1[...] = jnp.zeros_like(s1)
        s2[...] = jnp.zeros_like(s2)
        norm(0)
        norm(1)
        conv_row(0, (0, 1))
        norm(2)

    @pl.when(jnp.logical_and(step > 0, step < side - 1))
    def _():
        conv_row(step, (-1, 0, 1))
        norm(jnp.minimum(step + 2, side - 1))

    @pl.when(step == side - 1)
    def _():
        conv_row(side - 1, (-1, 0))
        core = core_ref[0]
        by_set = by_set_ref[...]
        split_halves(core, reorder(by_set, s1[...]), keep_ref, send_ref, 0)
        split_halves(core, reorder(by_set, s2[...]), keep_ref, send_ref, mid // 2)


def conv_stage(rows, core, y, mine, other, by_set, by_image, gain, shift, weight):
    places, count, mid = y.shape
    return pl.pallas_call(
        functools.partial(conv_kernel, rows),
        name="conv",
        grid=(SIDE,),
        in_specs=[SMEM] + [VMEM] * 8,
        out_specs=[VMEM] * 3,
        out_shape=[
            jax.ShapeDtypeStruct((places, count, mid), F32),
            jax.ShapeDtypeStruct((count, mid), F32),
            jax.ShapeDtypeStruct((count, mid), F32),
        ],
        scratch_shapes=[
            pltpu.VMEM((SIDE, SIDE, count, mid), BF16),
            pltpu.VMEM((count, mid), F32),
            pltpu.VMEM((count, mid), F32),
            pltpu.VMEM((count, mid), F32),
            pltpu.VMEM((count, mid), F32),
        ],
        compiler_params=params(16),
        cost_estimate=pl.CostEstimate(
            flops=2 * 361 * count * mid * mid,
            bytes_accessed=8 * places * count * mid + 2 * weight.size,
            transcendentals=0,
        ),
    )(core, y, mine, other, by_set, by_image, gain, shift, weight)


COLUMNS = 256


def center_kernel(gain_ref, shift_ref, w_ref, act_center_ref, center_ref):
    gain, shift = gain_ref[...], shift_ref[...]
    ratio = jnp.abs(shift) / gain
    value = jnp.maximum(shift, 0.0) + 0.4 * gain * jnp.exp(-ratio * (1.1 + 0.45 * ratio))
    value = value.astype(BF16)
    act_center_ref[...] = value.astype(F32)
    wide = dot32(jnp.broadcast_to(value, (16, value.shape[1])), w_ref[...])
    center_ref[...] = wide[:1]


def center_stage(gain, shift, weight):
    return pl.pallas_call(
        center_kernel,
        name="center",
        in_specs=[VMEM] * 3,
        out_specs=[VMEM] * 2,
        out_shape=[
            jax.ShapeDtypeStruct(gain.shape, F32),
            jax.ShapeDtypeStruct((1, weight.shape[1]), F32),
        ],
        compiler_params=pltpu.CompilerParams(vmem_limit_bytes=8 * 1024 * 1024),
        cost_estimate=pl.CostEstimate(
            flops=32 * weight.size, bytes_accessed=2 * weight.size, transcendentals=gain.size
        ),
    )(gain, shift, weight)


def expand_kernel(
    rows,
    core_ref,
    z_ref,
    mine_ref,
    other_ref,
    by_set_ref,
    by_image_ref,
    gain_ref,
    shift_ref,
    act_center_ref,
    center_ref,
    w_ref,
    e_ref,
    keep_ref,
    send_ref,
    act,
    sq_s,
):
    places, count, mid = z_ref.shape
    wide = w_ref.shape[1]
    core = core_ref[0]
    by_set = by_set_ref[...]
    scale, shift = scale_shift(
        core,
        mine_ref[...],
        other_ref[...],
        by_image_ref[...],
        gain_ref[...],
        shift_ref[...],
        rows,
    )
    total = jnp.zeros((count, mid), F32)
    for row in range(0, places, SIDE):
        a = z_ref[row : row + SIDE] * scale[None] + shift[None]
        a = jnp.maximum(a, 0.0).astype(BF16)
        act[row : row + SIDE] = a
        total += jnp.sum(a.astype(F32), 0)
    flat = act[...].reshape(places * count, mid)
    for j in range(0, wide, COLUMNS):
        e = dot32(flat, w_ref[:, j : j + COLUMNS]).reshape(places, count, COLUMNS)
        e_ref[:, :, j : j + COLUMNS] = e
        d = e - center_ref[:, j : j + COLUMNS][None]
        sq_s[:, j : j + COLUMNS] = jnp.sum(d * d, 0)
    total = total - places * act_center_ref[...]
    split_halves(core, reorder(by_set, total), keep_ref, send_ref, 0)
    split_halves(core, reorder(by_set, sq_s[...]), keep_ref, send_ref, mid // 2)


def expand_stage(
    rows, core, z, mine, other, by_set, by_image, gain, shift, act_center, center, weight
):
    places, count, mid = z.shape
    wide = weight.shape[1]
    sums = (mid + wide) // 2
    return pl.pallas_call(
        functools.partial(expand_kernel, rows),
        name="expand",
        in_specs=[SMEM] + [VMEM] * 10,
        out_specs=[VMEM] * 3,
        out_shape=[
            jax.ShapeDtypeStruct((places, count, wide), F32),
            jax.ShapeDtypeStruct((count, sums), F32),
            jax.ShapeDtypeStruct((count, sums), F32),
        ],
        scratch_shapes=[
            pltpu.VMEM((places, count, mid), BF16),
            pltpu.VMEM((count, wide), F32),
        ],
        compiler_params=pltpu.CompilerParams(vmem_limit_bytes=16 * 1024 * 1024),
        cost_estimate=pl.CostEstimate(
            flops=2 * places * count * mid * wide,
            bytes_accessed=4 * places * count * (mid + wide),
            transcendentals=0,
        ),
    )(core, z, mine, other, by_set, by_image, gain, shift, act_center, center, weight)


def merge_kernel(
    rows,
    core_ref,
    e_ref,
    x_ref,
    mine_ref,
    other_ref,
    by_image_ref,
    gain_ref,
    shift_ref,
    act_center_ref,
    center_ref,
    w_ref,
    proj_ref,
    key_ref,
    copies_ref,
    scale_s,
    shift_s,
    pool,
):
    places, count, wide = e_ref.shape
    core, by_image = core_ref[0], by_image_ref[...]
    mine, other = mine_ref[...], other_ref[...]
    cut = w_ref.shape[0] // 2
    sums = join_halves(core, mine[:, :cut], other[:, :cut]) + rows * act_center_ref[...]
    squares = join_halves(core, mine[:, cut:], other[:, cut:])
    three = dot32(pieces(sums), w_ref[...])
    sets = sums.shape[0]
    average = (three[:sets] + (three[sets : 2 * sets] + three[2 * sets :])) / rows
    away = average - center_ref[...]
    spread = squares / rows - away * away
    scale = lax.rsqrt(spread + EPS) * gain_ref[...]
    scale_s[...] = reorder(by_image, scale)
    shift_s[...] = reorder(by_image, shift_ref[...] - average * scale)
    for j in range(0, wide, COLUMNS):
        cols = slice(j, j + COLUMNS)
        sc, sh = scale_s[:, cols], shift_s[:, cols]
        total = jnp.zeros((count, COLUMNS), F32)
        for place in range(places):
            y = e_ref[place, :, cols] * sc + sh + x_ref[place, :, cols].astype(F32)
            total += jnp.maximum(y, 0.0)
        pool[:, cols] = total
    pooled = (pool[...] / places).astype(BF16)
    u = dot32(pooled, proj_ref[...])
    key = (u * lax.rsqrt(jnp.sum(u * u, 1, keepdims=True) + UNIT_EPS)).astype(BF16)
    key_ref[...] = key
    copies_ref[...] = jnp.broadcast_to(key[None], copies_ref.shape)


def merge_stage(
    rows, core, peers, e, x, mine, other, by_image, gain, shift, act_center, center, weight, proj
):
    places, count, wide = e.shape
    feat = proj.shape[1]
    return pl.pallas_call(
        functools.partial(merge_kernel, rows),
        name="merge",
        in_specs=[SMEM] + [VMEM] * 11,
        out_specs=[VMEM] * 2,
        out_shape=[
            jax.ShapeDtypeStruct((count, feat), BF16),
            jax.ShapeDtypeStruct((peers, count, feat), BF16),
        ],
        scratch_shapes=[
            pltpu.VMEM((count, wide), F32),
            pltpu.VMEM((count, wide), F32),
            pltpu.VMEM((count, wide), F32),
        ],
        compiler_params=pltpu.CompilerParams(vmem_limit_bytes=16 * 1024 * 1024),
        cost_estimate=pl.CostEstimate(
            flops=8 * places * count * wide,
            bytes_accessed=2 * x.size + 4 * e.size,
            transcendentals=0,
        ),
    )(core, e, x, mine, other, by_image, gain, shift, act_center, center, weight, proj)


def negative_kernel(factor, q_ref, k_ref, out_ref):
    @pl.when(pl.program_id(0) == 0)
    def _():
        out_ref[...] = jnp.zeros_like(out_ref)

    keys = k_ref[...]
    wide = keys.astype(F32)
    norm = lax.rsqrt(jnp.sum(wide * wide, 1, keepdims=True) + UNIT_EPS) * factor
    score = lax.dot_general(
        keys, q_ref[...], (((1,), (1,)), ((), ())), preferred_element_type=F32
    )
    out_ref[...] += jnp.sum(jnp.exp2(score * norm), 0, keepdims=True)


def negative_stage(queries, keys, part, parts):
    count, feat = queries.shape
    total = keys.shape[0] // parts
    block = math.gcd(total, 2048)
    steps = total // block
    return pl.pallas_call(
        functools.partial(negative_kernel, math.log2(math.e) / TEMP),
        name="negative",
        grid=(steps,),
        in_specs=[VMEM, pl.BlockSpec((block, feat), lambda i: (i + part * steps, 0))],
        out_specs=pl.BlockSpec((1, count), lambda i: (0, 0)),
        out_shape=jax.ShapeDtypeStruct((1, count), F32),
        compiler_params=params(8),
        cost_estimate=pl.CostEstimate(
            flops=2 * total * count * feat,
            bytes_accessed=2 * total * feat,
            transcendentals=total * count,
        ),
    )(queries, keys)


def loss_kernel(table_ref, u_ref, pos_ref, neg_ref, loss_ref):
    logits = lax.dot_general(
        table_ref[...], u_ref[...], (((1,), (1,)), ((), ())), preferred_element_type=F32
    )
    row = lax.broadcasted_iota(jnp.int32, logits.shape, 0)
    picked = jnp.sum(jnp.where(row == pos_ref[...], logits, 0.0), 0, keepdims=True) / TEMP
    loss_ref[...] = jnp.log(jnp.exp(picked) + neg_ref[...]) - picked


def loss_stage(table, units, positive, negatives):
    return pl.pallas_call(
        loss_kernel,
        name="loss",
        in_specs=[VMEM] * 4,
        out_specs=VMEM,
        out_shape=jax.ShapeDtypeStruct(positive.shape, F32),
        compiler_params=pltpu.CompilerParams(vmem_limit_bytes=8 * 1024 * 1024),
    )(table, units, positive, negatives)


def unit_rows(values):
    as_float = values.astype(F32)
    return (
        as_float * lax.rsqrt(jnp.sum(as_float * as_float, -1, keepdims=True) + UNIT_EPS)
    ).astype(BF16)


RING = 4


def swap_core():
    return [(i, i ^ 1) for i in range(2 * RING * RING)]


def ring_swap(k, flip):
    pairs = []
    for i in range(2 * RING * RING):
        x, z, c = i // (2 * RING), (i // 2) % RING, i % 2
        if (c == 1) != flip:
            x = x ^ k
        else:
            z = z ^ k
        pairs.append((i, (x * RING + z) * 2 + c))
    return pairs


def queue_swap(values, k):
    return lax.ppermute(values, "queue", [(i, i ^ k) for i in range(RING)])


def reduce_sets(keep, send, side_work, side_input, wire):
    total = keep + lax.ppermute(send, "dp", swap_core())
    for turn, work in enumerate(side_work):
        parts = []
        sent = total.astype(wire)
        for k in (1, 2, 3):
            parts.append(lax.ppermute(sent, "dp", ring_swap(k, turn == 1)).astype(F32))
        held, free = work(lax.optimization_barrier((side_input, total))[0])
        parts, held = lax.optimization_barrier((parts, held))
        side_input = (held, free)
        total = (total + parts[0]) + (parts[1] + parts[2])
    return total, lax.ppermute(total, "dp", swap_core()), side_input


def on_device(
    features,
    shuffle,
    positive,
    queries,
    queue_keys,
    reduce_weight,
    gain_one,
    shift_one,
    w_spatial,
    gain_two,
    shift_two,
    w_expand,
    gain_three,
    shift_three,
    w_project,
):
    count, places, _ = features.shape
    peers = lax.axis_size("dp")
    me = lax.axis_index("dp").astype(jnp.int32).reshape(1)
    core = jnp.bitwise_and(me, 1)
    rows = count * places
    x = jnp.transpose(features, (1, 0, 2))
    gain_two, shift_two = gain_two[None], shift_two[None]

    def negative_one(state):
        here, gain, shift = state
        here = unit_rows(here)
        centers = center_stage(gain, shift, w_expand)
        return (here, negative_stage(here, queue_keys, 0, 2), centers), None

    def negative_two(state):
        here, sums, centers = state[0]
        return (here, sums + negative_stage(here, queue_keys, 1, 2), centers), None

    def nothing(state):
        return None, None

    first = queue_swap(queries, 1)
    y, keep, send, by_set, by_image, x = reduce_stage(me, x, reduce_weight, shuffle)
    pair = jnp.concatenate([queries, first], 0)
    mine, other, _ = reduce_sets(keep, send, (nothing, nothing), None, F32)
    asked = jnp.concatenate([pair, queue_swap(pair, 3)], 0)
    z, keep, send = conv_stage(
        rows, core, y, mine, other, by_set, by_image, gain_one[None], shift_one[None], w_spatial
    )
    mine, other, ((units, sums, centers), _) = reduce_sets(
        keep, send, (negative_one, negative_two), (asked, gain_two, shift_two), F32
    )
    told = queue_swap(sums[:, 2 * count :], 3)
    e, keep, send = expand_stage(
        rows, core, z, mine, other, by_set, by_image, gain_two, shift_two, *centers, w_expand
    )
    mine, other, _ = reduce_sets(keep, send, (nothing, nothing), None, BF16)
    sums = sums[:, : 2 * count] + told
    told = queue_swap(sums[:, count:], 1)
    key_rows, copies = merge_stage(
        rows,
        core,
        peers,
        e,
        x,
        mine,
        other,
        by_image,
        gain_three[None],
        shift_three[None],
        *centers,
        w_expand,
        w_project,
    )
    table = lax.all_to_all(copies, "dp", split_axis=0, concat_axis=0, tiled=True)
    table = table.reshape(peers * count, -1)
    negatives = sums[:, :count] + told
    loss_vals = loss_stage(table, units[:count], positive.reshape(1, count), negatives)
    return (loss_vals.reshape(count), key_rows)


def solution(mesh):
    placed = (
        P(("queue", "dp"), None, None),
        P("queue", None),
        P(("queue", "dp")),
        P(("queue", "dp"), None),
        P("queue", None),
    ) + (P(),) * 10
    return jax.shard_map(
        on_device,
        mesh=mesh,
        in_specs=placed,
        out_specs=(P(("queue", "dp")), P(("queue", "dp"), None)),
        check_vma=False,
    )
```

```python
import functools
import math

import jax
import jax.numpy as jnp
from jax import lax
from jax.experimental import pallas as pl
from jax.experimental.pallas import tpu as pltpu
from jax.sharding import PartitionSpec as P


SIDE = 7
EPS = 1e-05
UNIT_EPS = 1e-06
TEMP = 0.2
F32 = jnp.float32
BF16 = jnp.bfloat16
VMEM = pl.BlockSpec(memory_space=pltpu.VMEM)
SMEM = pl.BlockSpec(memory_space=pltpu.SMEM)


def params(limit_mib):
    return pltpu.CompilerParams(
        dimension_semantics=("arbitrary",), vmem_limit_bytes=limit_mib * 1024 * 1024
    )


def dot32(a, b):
    return jnp.dot(a, b, preferred_element_type=F32)


def pieces(values):
    high = values.astype(BF16)
    rest = values - high.astype(F32)
    middle = rest.astype(BF16)
    low = (rest - middle.astype(F32)).astype(BF16)
    return jnp.concatenate([high, middle, low], 0)


def set_onehots(me, shuffle, count):
    total = shuffle.shape[1]
    image = lax.broadcasted_iota(jnp.int32, (count, total), 0) + me * count
    here = (shuffle == image).astype(F32)
    slot = lax.broadcasted_iota(jnp.int32, (total, total // count), 0)
    low = lax.broadcasted_iota(jnp.int32, (total, total // count), 1) * count
    inside = jnp.logical_and(slot >= low, slot < low + count)
    by_image = dot32(here.astype(BF16), inside.astype(F32).astype(BF16))
    by_set = jnp.transpose(by_image, (1, 0))
    return [jnp.concatenate([p] * 3, 1).astype(BF16) for p in (by_set, by_image)]


def reorder(onehot, values):
    return dot32(onehot, pieces(values))


def split_halves(core, values, keep_ref, send_ref, start):
    half = values.shape[1] // 2
    low, high = values[:, :half], values[:, half:]
    keep_ref[:, start : start + half] = jnp.where(core == 0, low, high)
    send_ref[:, start : start + half] = jnp.where(core == 0, high, low)


def join_halves(core, mine, other):
    low = jnp.where(core == 0, mine, other)
    high = jnp.where(core == 0, other, mine)
    return jnp.concatenate([low, high], 1)


CHUNKS = ((0, 7), (7, 14), (21, 28))


def reduce_kernel(
    me_ref,
    core_ref,
    x_hbm,
    w_hbm,
    shuffle_hbm,
    y_ref,
    keep_ref,
    send_ref,
    by_set_ref,
    by_image_ref,
    x_ref,
    w_ref,
    shuffle_ref,
    sems,
):
    _, count, channels = x_ref.shape
    mid = w_ref.shape[1]
    shuffle_copy = pltpu.make_async_copy(shuffle_hbm, shuffle_ref, sems.at[len(CHUNKS) + 1])
    shuffle_copy.start()
    weight_copy = pltpu.make_async_copy(w_hbm, w_ref, sems.at[0])
    weight_copy.start()
    copies = []
    for n, (first, size) in enumerate(CHUNKS):
        part = pl.ds(first, size)
        copies.append(pltpu.make_async_copy(x_hbm.at[part], x_ref.at[part], sems.at[n + 1]))
        copies[-1].start()
    shuffle_copy.wait()
    by_set, by_image = set_onehots(me_ref[0], shuffle_ref[...], count)
    by_set_ref[...] = by_set
    by_image_ref[...] = by_image
    weight_copy.wait()
    s1 = jnp.zeros((count, mid), F32)
    s2 = jnp.zeros((count, mid), F32)
    for (first, size), copy in zip(CHUNKS, copies):
        copy.wait()
        part = pl.ds(first, size)
        y = dot32(x_ref[part].reshape(size * count, channels), w_ref[...])
        y = y.reshape(size, count, mid)
        y_ref[part] = y
        s1 += jnp.sum(y, 0)
        s2 += jnp.sum(y * y, 0)
    core = core_ref[0]
    split_halves(core, reorder(by_set, s1), keep_ref, send_ref, 0)
    split_halves(core, reorder(by_set, s2), keep_ref, send_ref, mid // 2)


def reduce_stage(me, core, x, weight, shuffle):
    places, count, channels = x.shape
    mid = weight.shape[1]
    sets = shuffle.shape[1] // count
    hbm = pl.BlockSpec(memory_space=pltpu.HBM)
    return pl.pallas_call(
        reduce_kernel,
        name="reduce",
        in_specs=[SMEM, SMEM, hbm, hbm, hbm],
        out_specs=[VMEM] * 6,
        out_shape=[
            jax.ShapeDtypeStruct((places, count, mid), F32),
            jax.ShapeDtypeStruct((count, mid), F32),
            jax.ShapeDtypeStruct((count, mid), F32),
            jax.ShapeDtypeStruct((sets, 3 * count), BF16),
            jax.ShapeDtypeStruct((count, 3 * sets), BF16),
            jax.ShapeDtypeStruct(x.shape, x.dtype),
        ],
        scratch_shapes=[
            pltpu.VMEM(weight.shape, weight.dtype),
            pltpu.VMEM(shuffle.shape, shuffle.dtype),
            pltpu.SemaphoreType.DMA((len(CHUNKS) + 2,)),
        ],
        compiler_params=pltpu.CompilerParams(vmem_limit_bytes=24 * 1024 * 1024),
        cost_estimate=pl.CostEstimate(
            flops=2 * places * count * channels * mid,
            bytes_accessed=2 * x.size + 4 * places * count * mid,
            transcendentals=0,
        ),
    )(me, core, *[pltpu.with_memory_space_constraint(v, pltpu.HBM) for v in (x, weight, shuffle)])


def scale_shift(core, mine, other, onehot, gain, shift, rows):
    half = mine.shape[1] // 2
    total1 = join_halves(core, mine[:, :half], other[:, :half])
    total2 = join_halves(core, mine[:, half:], other[:, half:])
    average = total1 / rows
    spread = total2 / rows - average * average
    scale = lax.rsqrt(spread + EPS) * gain
    return reorder(onehot, scale), reorder(onehot, shift - average * scale)


def conv_kernel(
    rows,
    core_ref,
    y_ref,
    mine_ref,
    other_ref,
    by_set_ref,
    by_image_ref,
    gain_ref,
    shift_ref,
    w_ref,
    z_ref,
    keep_ref,
    send_ref,
    act,
    scale_s,
    shift_s,
    s1,
    s2,
):
    step = pl.program_id(0)
    side = SIDE
    _, count, mid = y_ref.shape

    def norm(row):
        a = y_ref[pl.ds(row * side, side)] * scale_s[...][None] + shift_s[...][None]
        act[row] = jnp.maximum(a, 0.0).astype(BF16)

    def conv_row(row, dys):
        for dx in (0, -1, 1):
            lo, hi = max(0, -dx), side - max(0, dx)
            window = [act[row + dy, lo + dx : hi + dx].reshape((hi - lo) * count, mid) for dy in dys]
            weight = [w_ref[3 * (dy + 1) + dx + 1] for dy in dys]
            part = dot32(jnp.concatenate(window, 1), jnp.concatenate(weight, 0))
            part = part.reshape(hi - lo, count, mid)
            if dx == 0:
                z_ref[pl.ds(row * side, side)] = part
            else:
                z_ref[pl.ds(row * side + lo, hi - lo)] += part
        z = z_ref[pl.ds(row * side, side)]
        s1[...] += jnp.sum(z, 0)
        s2[...] += jnp.sum(z * z, 0)

    @pl.when(step == 0)
    def _():
        scale, shift = scale_shift(
            core_ref[0],
            mine_ref[...],
            other_ref[...],
            by_image_ref[...],
            gain_ref[...],
            shift_ref[...],
            rows,
        )
        scale_s[...] = scale
        shift_s[...] = shift
        s1[...] = jnp.zeros_like(s1)
        s2[...] = jnp.zeros_like(s2)
        norm(0)
        norm(1)
        conv_row(0, (0, 1))
        norm(2)

    @pl.when(jnp.logical_and(step > 0, step < side - 1))
    def _():
        conv_row(step, (-1, 0, 1))
        norm(jnp.minimum(step + 2, side - 1))

    @pl.when(step == side - 1)
    def _():
        conv_row(side - 1, (-1, 0))
        core = core_ref[0]
        by_set = by_set_ref[...]
        split_halves(core, reorder(by_set, s1[...]), keep_ref, send_ref, 0)
        split_halves(core, reorder(by_set, s2[...]), keep_ref, send_ref, mid // 2)


def conv_stage(rows, core, y, mine, other, by_set, by_image, gain, shift, weight):
    places, count, mid = y.shape
    return pl.pallas_call(
        functools.partial(conv_kernel, rows),
        name="conv",
        grid=(SIDE,),
        in_specs=[SMEM] + [VMEM] * 8,
        out_specs=[VMEM] * 3,
        out_shape=[
            jax.ShapeDtypeStruct((places, count, mid), F32),
            jax.ShapeDtypeStruct((count, mid), F32),
            jax.ShapeDtypeStruct((count, mid), F32),
        ],
        scratch_shapes=[
            pltpu.VMEM((SIDE, SIDE, count, mid), BF16),
            pltpu.VMEM((count, mid), F32),
            pltpu.VMEM((count, mid), F32),
            pltpu.VMEM((count, mid), F32),
            pltpu.VMEM((count, mid), F32),
        ],
        compiler_params=params(16),
        cost_estimate=pl.CostEstimate(
            flops=2 * 361 * count * mid * mid,
            bytes_accessed=8 * places * count * mid + 2 * weight.size,
            transcendentals=0,
        ),
    )(core, y, mine, other, by_set, by_image, gain, shift, weight)


COLUMNS = 256


def center_kernel(gain_ref, shift_ref, w_ref, act_center_ref, center_ref):
    gain, shift = gain_ref[...], shift_ref[...]
    ratio = jnp.abs(shift) / gain
    value = jnp.maximum(shift, 0.0) + 0.4 * gain * jnp.exp(-ratio * (1.1 + 0.45 * ratio))
    value = value.astype(BF16)
    act_center_ref[...] = value.astype(F32)
    wide = dot32(jnp.broadcast_to(value, (16, value.shape[1])), w_ref[...])
    center_ref[...] = wide[:1]


def center_stage(gain, shift, weight):
    return pl.pallas_call(
        center_kernel,
        name="center",
        in_specs=[VMEM] * 3,
        out_specs=[VMEM] * 2,
        out_shape=[
            jax.ShapeDtypeStruct(gain.shape, F32),
            jax.ShapeDtypeStruct((1, weight.shape[1]), F32),
        ],
        compiler_params=pltpu.CompilerParams(vmem_limit_bytes=8 * 1024 * 1024),
        cost_estimate=pl.CostEstimate(
            flops=32 * weight.size, bytes_accessed=2 * weight.size, transcendentals=gain.size
        ),
    )(gain, shift, weight)


def expand_kernel(
    rows,
    core_ref,
    z_ref,
    mine_ref,
    other_ref,
    by_set_ref,
    by_image_ref,
    gain_ref,
    shift_ref,
    act_center_ref,
    center_ref,
    w_ref,
    e_ref,
    keep_ref,
    send_ref,
    act,
    sq_s,
):
    places, count, mid = z_ref.shape
    wide = w_ref.shape[1]
    core = core_ref[0]
    by_set = by_set_ref[...]
    scale, shift = scale_shift(
        core,
        mine_ref[...],
        other_ref[...],
        by_image_ref[...],
        gain_ref[...],
        shift_ref[...],
        rows,
    )
    total = jnp.zeros((count, mid), F32)
    for row in range(0, places, SIDE):
        a = z_ref[row : row + SIDE] * scale[None] + shift[None]
        a = jnp.maximum(a, 0.0).astype(BF16)
        act[row : row + SIDE] = a
        total += jnp.sum(a.astype(F32), 0)
    flat = act[...].reshape(places * count, mid)
    for j in range(0, wide, COLUMNS):
        e = dot32(flat, w_ref[:, j : j + COLUMNS]).reshape(places, count, COLUMNS)
        e_ref[:, :, j : j + COLUMNS] = e
        d = e - center_ref[:, j : j + COLUMNS][None]
        sq_s[:, j : j + COLUMNS] = jnp.sum(d * d, 0)
    total = total - places * act_center_ref[...]
    split_halves(core, reorder(by_set, total), keep_ref, send_ref, 0)
    split_halves(core, reorder(by_set, sq_s[...]), keep_ref, send_ref, mid // 2)


def expand_stage(
    rows, core, z, mine, other, by_set, by_image, gain, shift, act_center, center, weight
):
    places, count, mid = z.shape
    wide = weight.shape[1]
    sums = (mid + wide) // 2
    return pl.pallas_call(
        functools.partial(expand_kernel, rows),
        name="expand",
        in_specs=[SMEM] + [VMEM] * 10,
        out_specs=[VMEM] * 3,
        out_shape=[
            jax.ShapeDtypeStruct((places, count, wide), F32),
            jax.ShapeDtypeStruct((count, sums), F32),
            jax.ShapeDtypeStruct((count, sums), F32),
        ],
        scratch_shapes=[
            pltpu.VMEM((places, count, mid), BF16),
            pltpu.VMEM((count, wide), F32),
        ],
        compiler_params=pltpu.CompilerParams(vmem_limit_bytes=16 * 1024 * 1024),
        cost_estimate=pl.CostEstimate(
            flops=2 * places * count * mid * wide,
            bytes_accessed=4 * places * count * (mid + wide),
            transcendentals=0,
        ),
    )(core, z, mine, other, by_set, by_image, gain, shift, act_center, center, weight)


def merge_kernel(
    rows,
    core_ref,
    e_ref,
    x_ref,
    mine_ref,
    other_ref,
    by_image_ref,
    gain_ref,
    shift_ref,
    act_center_ref,
    center_ref,
    w_ref,
    proj_ref,
    key_ref,
    copies_ref,
    scale_s,
    shift_s,
    pool,
):
    places, count, wide = e_ref.shape
    core, by_image = core_ref[0], by_image_ref[...]
    mine, other = mine_ref[...], other_ref[...]
    cut = w_ref.shape[0] // 2
    sums = join_halves(core, mine[:, :cut], other[:, :cut]) + rows * act_center_ref[...]
    squares = join_halves(core, mine[:, cut:], other[:, cut:])
    three = dot32(pieces(sums), w_ref[...])
    sets = sums.shape[0]
    average = (three[:sets] + (three[sets : 2 * sets] + three[2 * sets :])) / rows
    away = average - center_ref[...]
    spread = squares / rows - away * away
    scale = lax.rsqrt(spread + EPS) * gain_ref[...]
    scale_s[...] = reorder(by_image, scale)
    shift_s[...] = reorder(by_image, shift_ref[...] - average * scale)
    for j in range(0, wide, COLUMNS):
        cols = slice(j, j + COLUMNS)
        sc, sh = scale_s[:, cols], shift_s[:, cols]
        total = jnp.zeros((count, COLUMNS), F32)
        for place in range(places):
            y = e_ref[place, :, cols] * sc + sh + x_ref[place, :, cols].astype(F32)
            total += jnp.maximum(y, 0.0)
        pool[:, cols] = total
    pooled = (pool[...] / places).astype(BF16)
    u = dot32(pooled, proj_ref[...])
    key = (u * lax.rsqrt(jnp.sum(u * u, 1, keepdims=True) + UNIT_EPS)).astype(BF16)
    key_ref[...] = key
    copies_ref[...] = jnp.broadcast_to(key[None], copies_ref.shape)


def merge_stage(
    rows, core, peers, e, x, mine, other, by_image, gain, shift, act_center, center, weight, proj
):
    places, count, wide = e.shape
    feat = proj.shape[1]
    return pl.pallas_call(
        functools.partial(merge_kernel, rows),
        name="merge",
        in_specs=[SMEM] + [VMEM] * 11,
        out_specs=[VMEM] * 2,
        out_shape=[
            jax.ShapeDtypeStruct((count, feat), BF16),
            jax.ShapeDtypeStruct((peers, count, feat), BF16),
        ],
        scratch_shapes=[
            pltpu.VMEM((count, wide), F32),
            pltpu.VMEM((count, wide), F32),
            pltpu.VMEM((count, wide), F32),
        ],
        compiler_params=pltpu.CompilerParams(vmem_limit_bytes=16 * 1024 * 1024),
        cost_estimate=pl.CostEstimate(
            flops=8 * places * count * wide,
            bytes_accessed=2 * x.size + 4 * e.size,
            transcendentals=0,
        ),
    )(core, e, x, mine, other, by_image, gain, shift, act_center, center, weight, proj)


def negative_kernel(factor, q_ref, k_ref, out_ref):
    @pl.when(pl.program_id(0) == 0)
    def _():
        out_ref[...] = jnp.zeros_like(out_ref)

    keys = k_ref[...]
    wide = keys.astype(F32)
    norm = lax.rsqrt(jnp.sum(wide * wide, 1, keepdims=True) + UNIT_EPS) * factor
    score = lax.dot_general(
        keys, q_ref[...], (((1,), (1,)), ((), ())), preferred_element_type=F32
    )
    out_ref[...] += jnp.sum(jnp.exp2(score * norm), 0, keepdims=True)


def negative_stage(queries, keys, part, parts):
    count, feat = queries.shape
    total = keys.shape[0] // parts
    block = math.gcd(total, 2048)
    steps = total // block
    return pl.pallas_call(
        functools.partial(negative_kernel, math.log2(math.e) / TEMP),
        name="negative",
        grid=(steps,),
        in_specs=[VMEM, pl.BlockSpec((block, feat), lambda i: (i + part * steps, 0))],
        out_specs=pl.BlockSpec((1, count), lambda i: (0, 0)),
        out_shape=jax.ShapeDtypeStruct((1, count), F32),
        compiler_params=params(8),
        cost_estimate=pl.CostEstimate(
            flops=2 * total * count * feat,
            bytes_accessed=2 * total * feat,
            transcendentals=total * count,
        ),
    )(queries, keys)


def loss_kernel(table_ref, u_ref, pos_ref, neg_ref, loss_ref):
    logits = lax.dot_general(
        table_ref[...], u_ref[...], (((1,), (1,)), ((), ())), preferred_element_type=F32
    )
    row = lax.broadcasted_iota(jnp.int32, logits.shape, 0)
    picked = jnp.sum(jnp.where(row == pos_ref[...], logits, 0.0), 0, keepdims=True) / TEMP
    loss_ref[...] = jnp.log(jnp.exp(picked) + neg_ref[...]) - picked


def loss_stage(table, units, positive, negatives):
    return pl.pallas_call(
        loss_kernel,
        name="loss",
        in_specs=[VMEM] * 4,
        out_specs=VMEM,
        out_shape=jax.ShapeDtypeStruct(positive.shape, F32),
        compiler_params=pltpu.CompilerParams(vmem_limit_bytes=8 * 1024 * 1024),
    )(table, units, positive, negatives)


def unit_rows(values):
    as_float = values.astype(F32)
    return (
        as_float * lax.rsqrt(jnp.sum(as_float * as_float, -1, keepdims=True) + UNIT_EPS)
    ).astype(BF16)


RING = 4


def swap_core():
    return [(i, i ^ 1) for i in range(2 * RING * RING)]


def mixed(v):
    return (v ^ (v >> 1)) & 1


def ring_swap(k, flip):
    pairs = []
    for i in range(2 * RING * RING):
        x, z, c = i // (2 * RING), (i // 2) % RING, i % 2
        half = c ^ mixed(x) ^ mixed(z)
        if (half == 1) != flip:
            x = x ^ k
        else:
            z = z ^ k
        pairs.append((i, (x * RING + z) * 2 + (half ^ mixed(x) ^ mixed(z))))
    return pairs


def queue_swap(values, k):
    return lax.ppermute(values, "queue", [(i, i ^ k) for i in range(RING)])


def reduce_sets(keep, send, side_work, side_input, wire):
    total = keep + lax.ppermute(send, "dp", swap_core())
    for turn, work in enumerate(side_work):
        parts = []
        sent = total.astype(wire)
        for k in (1, 2, 3):
            parts.append(lax.ppermute(sent, "dp", ring_swap(k, turn == 1)).astype(F32))
        held, free = work(lax.optimization_barrier((side_input, total))[0])
        parts, held = lax.optimization_barrier((parts, held))
        side_input = (held, free)
        total = (total + parts[0]) + (parts[1] + parts[2])
    return total, lax.ppermute(total, "dp", swap_core()), side_input


def on_device(
    features,
    shuffle,
    positive,
    queries,
    queue_keys,
    reduce_weight,
    gain_one,
    shift_one,
    w_spatial,
    gain_two,
    shift_two,
    w_expand,
    gain_three,
    shift_three,
    w_project,
):
    count, places, _ = features.shape
    peers = lax.axis_size("dp")
    me = lax.axis_index("dp").astype(jnp.int32)
    core = me ^ mixed(me >> 3) ^ mixed((me >> 1) & 3)
    core = jnp.bitwise_and(core, 1).reshape(1)
    rows = count * places
    x = jnp.transpose(features, (1, 0, 2))
    gain_two, shift_two = gain_two[None], shift_two[None]

    def negative_one(state):
        here, gain, shift = state
        here = unit_rows(here)
        centers = center_stage(gain, shift, w_expand)
        return (here, negative_stage(here, queue_keys, 0, 2), centers), None

    def negative_two(state):
        here, sums, centers = state[0]
        return (here, sums + negative_stage(here, queue_keys, 1, 2), centers), None

    def nothing(state):
        return None, None

    first = queue_swap(queries, 1)
    y, keep, send, by_set, by_image, x = reduce_stage(me.reshape(1), core, x, reduce_weight, shuffle)
    pair = jnp.concatenate([queries, first], 0)
    mine, other, _ = reduce_sets(keep, send, (nothing, nothing), None, F32)
    asked = jnp.concatenate([pair, queue_swap(pair, 3)], 0)
    z, keep, send = conv_stage(
        rows, core, y, mine, other, by_set, by_image, gain_one[None], shift_one[None], w_spatial
    )
    mine, other, ((units, sums, centers), _) = reduce_sets(
        keep, send, (negative_one, negative_two), (asked, gain_two, shift_two), F32
    )
    told = queue_swap(sums[:, 2 * count :], 3)
    e, keep, send = expand_stage(
        rows, core, z, mine, other, by_set, by_image, gain_two, shift_two, *centers, w_expand
    )
    mine, other, _ = reduce_sets(keep, send, (nothing, nothing), None, BF16)
    sums = sums[:, : 2 * count] + told
    told = queue_swap(sums[:, count:], 1)
    key_rows, copies = merge_stage(
        rows,
        core,
        peers,
        e,
        x,
        mine,
        other,
        by_image,
        gain_three[None],
        shift_three[None],
        *centers,
        w_expand,
        w_project,
    )
    table = lax.all_to_all(copies, "dp", split_axis=0, concat_axis=0, tiled=True)
    table = table.reshape(peers * count, -1)
    negatives = sums[:, :count] + told
    loss_vals = loss_stage(table, units[:count], positive.reshape(1, count), negatives)
    return (loss_vals.reshape(count), key_rows)


def solution(mesh):
    placed = (
        P(("queue", "dp"), None, None),
        P("queue", None),
        P(("queue", "dp")),
        P(("queue", "dp"), None),
        P("queue", None),
    ) + (P(),) * 10
    return jax.shard_map(
        on_device,
        mesh=mesh,
        in_specs=placed,
        out_specs=(P(("queue", "dp")), P(("queue", "dp"), None)),
        check_vma=False,
    )
```

```python
import functools
import math

import jax
import jax.numpy as jnp
from jax import lax
from jax.experimental import pallas as pl
from jax.experimental.pallas import tpu as pltpu
from jax.sharding import PartitionSpec as P


SIDE = 7
EPS = 1e-05
UNIT_EPS = 1e-06
TEMP = 0.2
F32 = jnp.float32
BF16 = jnp.bfloat16
VMEM = pl.BlockSpec(memory_space=pltpu.VMEM)
SMEM = pl.BlockSpec(memory_space=pltpu.SMEM)


def params(limit_mib):
    return pltpu.CompilerParams(
        dimension_semantics=("arbitrary",), vmem_limit_bytes=limit_mib * 1024 * 1024
    )


def dot32(a, b):
    return jnp.dot(a, b, preferred_element_type=F32)


def pieces(values):
    high = values.astype(BF16)
    rest = values - high.astype(F32)
    middle = rest.astype(BF16)
    low = (rest - middle.astype(F32)).astype(BF16)
    return jnp.concatenate([high, middle, low], 0)


def set_onehots(me, shuffle, count):
    total = shuffle.shape[1]
    image = lax.broadcasted_iota(jnp.int32, (count, total), 0) + me * count
    here = (shuffle == image).astype(F32)
    slot = lax.broadcasted_iota(jnp.int32, (total, total // count), 0)
    low = lax.broadcasted_iota(jnp.int32, (total, total // count), 1) * count
    inside = jnp.logical_and(slot >= low, slot < low + count)
    by_image = dot32(here.astype(BF16), inside.astype(F32).astype(BF16))
    by_set = jnp.transpose(by_image, (1, 0))
    return [jnp.concatenate([p] * 3, 1).astype(BF16) for p in (by_set, by_image)]


def reorder(onehot, values):
    return dot32(onehot, pieces(values))


def split_halves(core, values, keep_ref, send_ref, start):
    half = values.shape[1] // 2
    low, high = values[:, :half], values[:, half:]
    keep_ref[:, start : start + half] = jnp.where(core == 0, low, high)
    send_ref[:, start : start + half] = jnp.where(core == 0, high, low)


def join_halves(core, mine, other):
    low = jnp.where(core == 0, mine, other)
    high = jnp.where(core == 0, other, mine)
    return jnp.concatenate([low, high], 1)


CHUNKS = ((0, 7), (7, 14), (21, 28))


def reduce_kernel(
    me_ref,
    core_ref,
    x_hbm,
    w_hbm,
    shuffle_hbm,
    next_hbm,
    y_ref,
    keep_ref,
    send_ref,
    by_set_ref,
    by_image_ref,
    x_ref,
    next_ref,
    w_ref,
    shuffle_ref,
    sems,
):
    _, count, channels = x_ref.shape
    mid = w_ref.shape[1]
    shuffle_copy = pltpu.make_async_copy(shuffle_hbm, shuffle_ref, sems.at[len(CHUNKS) + 1])
    shuffle_copy.start()
    weight_copy = pltpu.make_async_copy(w_hbm, w_ref, sems.at[0])
    weight_copy.start()
    copies = []
    for n, (first, size) in enumerate(CHUNKS):
        part = pl.ds(first, size)
        copies.append(pltpu.make_async_copy(x_hbm.at[part], x_ref.at[part], sems.at[n + 1]))
        copies[-1].start()
    next_copy = pltpu.make_async_copy(next_hbm, next_ref, sems.at[len(CHUNKS) + 2])
    next_copy.start()
    shuffle_copy.wait()
    by_set, by_image = set_onehots(me_ref[0], shuffle_ref[...], count)
    by_set_ref[...] = by_set
    by_image_ref[...] = by_image
    weight_copy.wait()
    s1 = jnp.zeros((count, mid), F32)
    s2 = jnp.zeros((count, mid), F32)
    for (first, size), copy in zip(CHUNKS, copies):
        copy.wait()
        part = pl.ds(first, size)
        y = dot32(x_ref[part].reshape(size * count, channels), w_ref[...])
        y = y.reshape(size, count, mid)
        y_ref[part] = y
        s1 += jnp.sum(y, 0)
        s2 += jnp.sum(y * y, 0)
    core = core_ref[0]
    split_halves(core, reorder(by_set, s1), keep_ref, send_ref, 0)
    split_halves(core, reorder(by_set, s2), keep_ref, send_ref, mid // 2)
    next_copy.wait()


def reduce_stage(me, core, x, weight, shuffle, later):
    places, count, channels = x.shape
    mid = weight.shape[1]
    sets = shuffle.shape[1] // count
    hbm = pl.BlockSpec(memory_space=pltpu.HBM)
    return pl.pallas_call(
        reduce_kernel,
        name="reduce",
        in_specs=[SMEM, SMEM, hbm, hbm, hbm, hbm],
        out_specs=[VMEM] * 7,
        out_shape=[
            jax.ShapeDtypeStruct((places, count, mid), F32),
            jax.ShapeDtypeStruct((count, mid), F32),
            jax.ShapeDtypeStruct((count, mid), F32),
            jax.ShapeDtypeStruct((sets, 3 * count), BF16),
            jax.ShapeDtypeStruct((count, 3 * sets), BF16),
            jax.ShapeDtypeStruct(x.shape, x.dtype),
            jax.ShapeDtypeStruct(later.shape, later.dtype),
        ],
        scratch_shapes=[
            pltpu.VMEM(weight.shape, weight.dtype),
            pltpu.VMEM(shuffle.shape, shuffle.dtype),
            pltpu.SemaphoreType.DMA((len(CHUNKS) + 3,)),
        ],
        compiler_params=pltpu.CompilerParams(vmem_limit_bytes=24 * 1024 * 1024),
        cost_estimate=pl.CostEstimate(
            flops=2 * places * count * channels * mid,
            bytes_accessed=2 * x.size + 4 * places * count * mid,
            transcendentals=0,
        ),
    )(
        me,
        core,
        *[pltpu.with_memory_space_constraint(v, pltpu.HBM) for v in (x, weight, shuffle, later)],
    )


def scale_shift(core, mine, other, onehot, gain, shift, rows):
    half = mine.shape[1] // 2
    total1 = join_halves(core, mine[:, :half], other[:, :half])
    total2 = join_halves(core, mine[:, half:], other[:, half:])
    average = total1 / rows
    spread = total2 / rows - average * average
    scale = lax.rsqrt(spread + EPS) * gain
    return reorder(onehot, scale), reorder(onehot, shift - average * scale)


def conv_kernel(
    rows,
    core_ref,
    y_ref,
    mine_ref,
    other_ref,
    by_set_ref,
    by_image_ref,
    gain_ref,
    shift_ref,
    w_ref,
    z_ref,
    keep_ref,
    send_ref,
    act,
    scale_s,
    shift_s,
    s1,
    s2,
):
    step = pl.program_id(0)
    side = SIDE
    _, count, mid = y_ref.shape

    def norm(row):
        a = y_ref[pl.ds(row * side, side)] * scale_s[...][None] + shift_s[...][None]
        act[row] = jnp.maximum(a, 0.0).astype(BF16)

    def conv_row(row, dys):
        for dx in (0, -1, 1):
            lo, hi = max(0, -dx), side - max(0, dx)
            window = [act[row + dy, lo + dx : hi + dx].reshape((hi - lo) * count, mid) for dy in dys]
            weight = [w_ref[3 * (dy + 1) + dx + 1] for dy in dys]
            part = dot32(jnp.concatenate(window, 1), jnp.concatenate(weight, 0))
            part = part.reshape(hi - lo, count, mid)
            if dx == 0:
                z_ref[pl.ds(row * side, side)] = part
            else:
                z_ref[pl.ds(row * side + lo, hi - lo)] += part
        z = z_ref[pl.ds(row * side, side)]
        s1[...] += jnp.sum(z, 0)
        s2[...] += jnp.sum(z * z, 0)

    @pl.when(step == 0)
    def _():
        scale, shift = scale_shift(
            core_ref[0],
            mine_ref[...],
            other_ref[...],
            by_image_ref[...],
            gain_ref[...],
            shift_ref[...],
            rows,
        )
        scale_s[...] = scale
        shift_s[...] = shift
        s1[...] = jnp.zeros_like(s1)
        s2[...] = jnp.zeros_like(s2)
        norm(0)
        norm(1)
        conv_row(0, (0, 1))
        norm(2)

    @pl.when(jnp.logical_and(step > 0, step < side - 1))
    def _():
        conv_row(step, (-1, 0, 1))
        norm(jnp.minimum(step + 2, side - 1))

    @pl.when(step == side - 1)
    def _():
        conv_row(side - 1, (-1, 0))
        core = core_ref[0]
        by_set = by_set_ref[...]
        split_halves(core, reorder(by_set, s1[...]), keep_ref, send_ref, 0)
        split_halves(core, reorder(by_set, s2[...]), keep_ref, send_ref, mid // 2)


def conv_stage(rows, core, y, mine, other, by_set, by_image, gain, shift, weight):
    places, count, mid = y.shape
    return pl.pallas_call(
        functools.partial(conv_kernel, rows),
        name="conv",
        grid=(SIDE,),
        in_specs=[SMEM] + [VMEM] * 8,
        out_specs=[VMEM] * 3,
        out_shape=[
            jax.ShapeDtypeStruct((places, count, mid), F32),
            jax.ShapeDtypeStruct((count, mid), F32),
            jax.ShapeDtypeStruct((count, mid), F32),
        ],
        scratch_shapes=[
            pltpu.VMEM((SIDE, SIDE, count, mid), BF16),
            pltpu.VMEM((count, mid), F32),
            pltpu.VMEM((count, mid), F32),
            pltpu.VMEM((count, mid), F32),
            pltpu.VMEM((count, mid), F32),
        ],
        compiler_params=params(16),
        cost_estimate=pl.CostEstimate(
            flops=2 * 361 * count * mid * mid,
            bytes_accessed=8 * places * count * mid + 2 * weight.size,
            transcendentals=0,
        ),
    )(core, y, mine, other, by_set, by_image, gain, shift, weight)


COLUMNS = 256


def center_kernel(gain_ref, shift_ref, w_ref, act_center_ref, center_ref):
    gain, shift = gain_ref[...], shift_ref[...]
    ratio = jnp.abs(shift) / gain
    value = jnp.maximum(shift, 0.0) + 0.4 * gain * jnp.exp(-ratio * (1.1 + 0.45 * ratio))
    value = value.astype(BF16)
    act_center_ref[...] = value.astype(F32)
    wide = dot32(jnp.broadcast_to(value, (16, value.shape[1])), w_ref[...])
    center_ref[...] = wide[:1]


def center_stage(gain, shift, weight):
    return pl.pallas_call(
        center_kernel,
        name="center",
        in_specs=[VMEM] * 3,
        out_specs=[VMEM] * 2,
        out_shape=[
            jax.ShapeDtypeStruct(gain.shape, F32),
            jax.ShapeDtypeStruct((1, weight.shape[1]), F32),
        ],
        compiler_params=pltpu.CompilerParams(vmem_limit_bytes=8 * 1024 * 1024),
        cost_estimate=pl.CostEstimate(
            flops=32 * weight.size, bytes_accessed=2 * weight.size, transcendentals=gain.size
        ),
    )(gain, shift, weight)


def expand_kernel(
    rows,
    core_ref,
    z_ref,
    mine_ref,
    other_ref,
    by_set_ref,
    by_image_ref,
    gain_ref,
    shift_ref,
    act_center_ref,
    center_ref,
    w_ref,
    e_ref,
    keep_ref,
    send_ref,
    act,
    sq_s,
):
    places, count, mid = z_ref.shape
    wide = w_ref.shape[1]
    core = core_ref[0]
    by_set = by_set_ref[...]
    scale, shift = scale_shift(
        core,
        mine_ref[...],
        other_ref[...],
        by_image_ref[...],
        gain_ref[...],
        shift_ref[...],
        rows,
    )
    total = jnp.zeros((count, mid), F32)
    for row in range(0, places, SIDE):
        a = z_ref[row : row + SIDE] * scale[None] + shift[None]
        a = jnp.maximum(a, 0.0).astype(BF16)
        act[row : row + SIDE] = a
        total += jnp.sum(a.astype(F32), 0)
    flat = act[...].reshape(places * count, mid)
    for j in range(0, wide, COLUMNS):
        e = dot32(flat, w_ref[:, j : j + COLUMNS]).reshape(places, count, COLUMNS)
        e_ref[:, :, j : j + COLUMNS] = e
        d = e - center_ref[:, j : j + COLUMNS][None]
        sq_s[:, j : j + COLUMNS] = jnp.sum(d * d, 0)
    total = total - places * act_center_ref[...]
    split_halves(core, reorder(by_set, total), keep_ref, send_ref, 0)
    split_halves(core, reorder(by_set, sq_s[...]), keep_ref, send_ref, mid // 2)


def expand_stage(
    rows, core, z, mine, other, by_set, by_image, gain, shift, act_center, center, weight
):
    places, count, mid = z.shape
    wide = weight.shape[1]
    sums = (mid + wide) // 2
    return pl.pallas_call(
        functools.partial(expand_kernel, rows),
        name="expand",
        in_specs=[SMEM] + [VMEM] * 10,
        out_specs=[VMEM] * 3,
        out_shape=[
            jax.ShapeDtypeStruct((places, count, wide), F32),
            jax.ShapeDtypeStruct((count, sums), F32),
            jax.ShapeDtypeStruct((count, sums), F32),
        ],
        scratch_shapes=[
            pltpu.VMEM((places, count, mid), BF16),
            pltpu.VMEM((count, wide), F32),
        ],
        compiler_params=pltpu.CompilerParams(vmem_limit_bytes=16 * 1024 * 1024),
        cost_estimate=pl.CostEstimate(
            flops=2 * places * count * mid * wide,
            bytes_accessed=4 * places * count * (mid + wide),
            transcendentals=0,
        ),
    )(core, z, mine, other, by_set, by_image, gain, shift, act_center, center, weight)


def merge_kernel(
    rows,
    core_ref,
    e_ref,
    x_ref,
    mine_ref,
    other_ref,
    by_image_ref,
    gain_ref,
    shift_ref,
    act_center_ref,
    center_ref,
    w_ref,
    proj_ref,
    key_ref,
    copies_ref,
    scale_s,
    shift_s,
    pool,
):
    places, count, wide = e_ref.shape
    core, by_image = core_ref[0], by_image_ref[...]
    mine, other = mine_ref[...], other_ref[...]
    cut = w_ref.shape[0] // 2
    sums = join_halves(core, mine[:, :cut], other[:, :cut]) + rows * act_center_ref[...]
    squares = join_halves(core, mine[:, cut:], other[:, cut:])
    three = dot32(pieces(sums), w_ref[...])
    sets = sums.shape[0]
    average = (three[:sets] + (three[sets : 2 * sets] + three[2 * sets :])) / rows
    away = average - center_ref[...]
    spread = squares / rows - away * away
    scale = lax.rsqrt(spread + EPS) * gain_ref[...]
    scale_s[...] = reorder(by_image, scale)
    shift_s[...] = reorder(by_image, shift_ref[...] - average * scale)
    for j in range(0, wide, COLUMNS):
        cols = slice(j, j + COLUMNS)
        sc, sh = scale_s[:, cols], shift_s[:, cols]
        total = jnp.zeros((count, COLUMNS), F32)
        for place in range(places):
            y = e_ref[place, :, cols] * sc + sh + x_ref[place, :, cols].astype(F32)
            total += jnp.maximum(y, 0.0)
        pool[:, cols] = total
    pooled = (pool[...] / places).astype(BF16)
    u = dot32(pooled, proj_ref[...])
    key = (u * lax.rsqrt(jnp.sum(u * u, 1, keepdims=True) + UNIT_EPS)).astype(BF16)
    key_ref[...] = key
    copies_ref[...] = jnp.broadcast_to(key[None], copies_ref.shape)


def merge_stage(
    rows, core, peers, e, x, mine, other, by_image, gain, shift, act_center, center, weight, proj
):
    places, count, wide = e.shape
    feat = proj.shape[1]
    return pl.pallas_call(
        functools.partial(merge_kernel, rows),
        name="merge",
        in_specs=[SMEM] + [VMEM] * 11,
        out_specs=[VMEM] * 2,
        out_shape=[
            jax.ShapeDtypeStruct((count, feat), BF16),
            jax.ShapeDtypeStruct((peers, count, feat), BF16),
        ],
        scratch_shapes=[
            pltpu.VMEM((count, wide), F32),
            pltpu.VMEM((count, wide), F32),
            pltpu.VMEM((count, wide), F32),
        ],
        compiler_params=pltpu.CompilerParams(vmem_limit_bytes=16 * 1024 * 1024),
        cost_estimate=pl.CostEstimate(
            flops=8 * places * count * wide,
            bytes_accessed=2 * x.size + 4 * e.size,
            transcendentals=0,
        ),
    )(core, e, x, mine, other, by_image, gain, shift, act_center, center, weight, proj)


def negative_kernel(factor, q_ref, k_ref, out_ref):
    @pl.when(pl.program_id(0) == 0)
    def _():
        out_ref[...] = jnp.zeros_like(out_ref)

    keys = k_ref[...]
    wide = keys.astype(F32)
    norm = lax.rsqrt(jnp.sum(wide * wide, 1, keepdims=True) + UNIT_EPS) * factor
    score = lax.dot_general(
        keys, q_ref[...], (((1,), (1,)), ((), ())), preferred_element_type=F32
    )
    out_ref[...] += jnp.sum(jnp.exp2(score * norm), 0, keepdims=True)


def negative_stage(queries, keys, part, parts):
    count, feat = queries.shape
    total = keys.shape[0] // parts
    block = math.gcd(total, 2048)
    steps = total // block
    return pl.pallas_call(
        functools.partial(negative_kernel, math.log2(math.e) / TEMP),
        name="negative",
        grid=(steps,),
        in_specs=[VMEM, pl.BlockSpec((block, feat), lambda i: (i + part * steps, 0))],
        out_specs=pl.BlockSpec((1, count), lambda i: (0, 0)),
        out_shape=jax.ShapeDtypeStruct((1, count), F32),
        compiler_params=params(8),
        cost_estimate=pl.CostEstimate(
            flops=2 * total * count * feat,
            bytes_accessed=2 * total * feat,
            transcendentals=total * count,
        ),
    )(queries, keys)


def loss_kernel(table_ref, u_ref, pos_ref, neg_ref, loss_ref):
    logits = lax.dot_general(
        table_ref[...], u_ref[...], (((1,), (1,)), ((), ())), preferred_element_type=F32
    )
    row = lax.broadcasted_iota(jnp.int32, logits.shape, 0)
    picked = jnp.sum(jnp.where(row == pos_ref[...], logits, 0.0), 0, keepdims=True) / TEMP
    loss_ref[...] = jnp.log(jnp.exp(picked) + neg_ref[...]) - picked


def loss_stage(table, units, positive, negatives):
    return pl.pallas_call(
        loss_kernel,
        name="loss",
        in_specs=[VMEM] * 4,
        out_specs=VMEM,
        out_shape=jax.ShapeDtypeStruct(positive.shape, F32),
        compiler_params=pltpu.CompilerParams(vmem_limit_bytes=8 * 1024 * 1024),
    )(table, units, positive, negatives)


def unit_rows(values):
    as_float = values.astype(F32)
    return (
        as_float * lax.rsqrt(jnp.sum(as_float * as_float, -1, keepdims=True) + UNIT_EPS)
    ).astype(BF16)


RING = 4


def swap_core():
    return [(i, i ^ 1) for i in range(2 * RING * RING)]


def mixed(v):
    return (v ^ (v >> 1)) & 1


def ring_swap(k, flip):
    pairs = []
    for i in range(2 * RING * RING):
        x, z, c = i // (2 * RING), (i // 2) % RING, i % 2
        half = c ^ mixed(x) ^ mixed(z)
        if (half == 1) != flip:
            x = x ^ k
        else:
            z = z ^ k
        pairs.append((i, (x * RING + z) * 2 + (half ^ mixed(x) ^ mixed(z))))
    return pairs


def queue_swap(values, k):
    return lax.ppermute(values, "queue", [(i, i ^ k) for i in range(RING)])


def reduce_sets(keep, send, side_work, side_input, wire):
    total = keep + lax.ppermute(send, "dp", swap_core())
    for turn, work in enumerate(side_work):
        parts = []
        sent = total.astype(wire)
        for k in (1, 2, 3):
            parts.append(lax.ppermute(sent, "dp", ring_swap(k, turn == 1)).astype(F32))
        held, free = work(lax.optimization_barrier((side_input, total))[0])
        parts, held = lax.optimization_barrier((parts, held))
        side_input = (held, free)
        total = (total + parts[0]) + (parts[1] + parts[2])
    return total, lax.ppermute(total, "dp", swap_core()), side_input


def on_device(
    features,
    shuffle,
    positive,
    queries,
    queue_keys,
    reduce_weight,
    gain_one,
    shift_one,
    w_spatial,
    gain_two,
    shift_two,
    w_expand,
    gain_three,
    shift_three,
    w_project,
):
    count, places, _ = features.shape
    peers = lax.axis_size("dp")
    me = lax.axis_index("dp").astype(jnp.int32)
    core = me ^ mixed(me >> 3) ^ mixed((me >> 1) & 3)
    core = jnp.bitwise_and(core, 1).reshape(1)
    rows = count * places
    x = jnp.transpose(features, (1, 0, 2))
    gain_two, shift_two = gain_two[None], shift_two[None]

    def negative_one(state):
        here, gain, shift = state
        here = unit_rows(here)
        centers = center_stage(gain, shift, w_expand)
        return (here, negative_stage(here, queue_keys, 0, 2), centers), None

    def negative_two(state):
        here, sums, centers = state[0]
        return (here, sums + negative_stage(here, queue_keys, 1, 2), centers), None

    def nothing(state):
        return None, None

    first = queue_swap(queries, 1)
    y, keep, send, by_set, by_image, x, w_spatial = reduce_stage(
        me.reshape(1), core, x, reduce_weight, shuffle, w_spatial
    )
    pair = jnp.concatenate([queries, first], 0)
    mine, other, _ = reduce_sets(keep, send, (nothing, nothing), None, F32)
    asked = jnp.concatenate([pair, queue_swap(pair, 3)], 0)
    z, keep, send = conv_stage(
        rows, core, y, mine, other, by_set, by_image, gain_one[None], shift_one[None], w_spatial
    )
    mine, other, ((units, sums, centers), _) = reduce_sets(
        keep, send, (negative_one, negative_two), (asked, gain_two, shift_two), F32
    )
    told = queue_swap(sums[:, 2 * count :], 3)
    e, keep, send = expand_stage(
        rows, core, z, mine, other, by_set, by_image, gain_two, shift_two, *centers, w_expand
    )
    mine, other, _ = reduce_sets(keep, send, (nothing, nothing), None, BF16)
    sums = sums[:, : 2 * count] + told
    told = queue_swap(sums[:, count:], 1)
    key_rows, copies = merge_stage(
        rows,
        core,
        peers,
        e,
        x,
        mine,
        other,
        by_image,
        gain_three[None],
        shift_three[None],
        *centers,
        w_expand,
        w_project,
    )
    table = lax.all_to_all(copies, "dp", split_axis=0, concat_axis=0, tiled=True)
    table = table.reshape(peers * count, -1)
    negatives = sums[:, :count] + told
    loss_vals = loss_stage(table, units[:count], positive.reshape(1, count), negatives)
    return (loss_vals.reshape(count), key_rows)


def solution(mesh):
    placed = (
        P(("queue", "dp"), None, None),
        P("queue", None),
        P(("queue", "dp")),
        P(("queue", "dp"), None),
        P("queue", None),
    ) + (P(),) * 10
    return jax.shard_map(
        on_device,
        mesh=mesh,
        in_specs=placed,
        out_specs=(P(("queue", "dp")), P(("queue", "dp"), None)),
        check_vma=False,
    )
```

```python
import functools
import math

import jax
import jax.numpy as jnp
from jax import lax
from jax.experimental import pallas as pl
from jax.experimental.pallas import tpu as pltpu
from jax.sharding import PartitionSpec as P


SIDE = 7
EPS = 1e-05
UNIT_EPS = 1e-06
TEMP = 0.2
F32 = jnp.float32
BF16 = jnp.bfloat16
VMEM = pl.BlockSpec(memory_space=pltpu.VMEM)
SMEM = pl.BlockSpec(memory_space=pltpu.SMEM)


def params(limit_mib):
    return pltpu.CompilerParams(
        dimension_semantics=("arbitrary",), vmem_limit_bytes=limit_mib * 1024 * 1024
    )


def dot32(a, b):
    return jnp.dot(a, b, preferred_element_type=F32)


def pieces(values):
    high = values.astype(BF16)
    rest = values - high.astype(F32)
    middle = rest.astype(BF16)
    low = (rest - middle.astype(F32)).astype(BF16)
    return jnp.concatenate([high, middle, low], 0)


def set_onehots(me, shuffle, count):
    total = shuffle.shape[1]
    image = lax.broadcasted_iota(jnp.int32, (count, total), 0) + me * count
    here = (shuffle == image).astype(F32)
    slot = lax.broadcasted_iota(jnp.int32, (total, total // count), 0)
    low = lax.broadcasted_iota(jnp.int32, (total, total // count), 1) * count
    inside = jnp.logical_and(slot >= low, slot < low + count)
    by_image = dot32(here.astype(BF16), inside.astype(F32).astype(BF16))
    by_set = jnp.transpose(by_image, (1, 0))
    return [jnp.concatenate([p] * 3, 1).astype(BF16) for p in (by_set, by_image)]


def reorder(onehot, values):
    return dot32(onehot, pieces(values))


def split_halves(core, values, keep_ref, send_ref, start):
    half = values.shape[1] // 2
    low, high = values[:, :half], values[:, half:]
    keep_ref[:, start : start + half] = jnp.where(core == 0, low, high)
    send_ref[:, start : start + half] = jnp.where(core == 0, high, low)


def join_halves(core, mine, other):
    low = jnp.where(core == 0, mine, other)
    high = jnp.where(core == 0, other, mine)
    return jnp.concatenate([low, high], 1)


CHUNKS = ((0, 7), (7, 14), (21, 28))


def reduce_kernel(
    me_ref,
    core_ref,
    x_hbm,
    w_hbm,
    shuffle_hbm,
    next_hbm,
    y_ref,
    keep_ref,
    send_ref,
    by_set_ref,
    by_image_ref,
    x_ref,
    next_ref,
    w_ref,
    shuffle_ref,
    sems,
):
    _, count, channels = x_ref.shape
    mid = w_ref.shape[1]
    shuffle_copy = pltpu.make_async_copy(shuffle_hbm, shuffle_ref, sems.at[len(CHUNKS) + 1])
    shuffle_copy.start()
    weight_copy = pltpu.make_async_copy(w_hbm, w_ref, sems.at[0])
    weight_copy.start()
    copies = []
    for n, (first, size) in enumerate(CHUNKS):
        part = pl.ds(first, size)
        copies.append(pltpu.make_async_copy(x_hbm.at[part], x_ref.at[part], sems.at[n + 1]))
        copies[-1].start()
    next_copy = pltpu.make_async_copy(next_hbm, next_ref, sems.at[len(CHUNKS) + 2])
    next_copy.start()
    shuffle_copy.wait()
    by_set, by_image = set_onehots(me_ref[0], shuffle_ref[...], count)
    by_set_ref[...] = by_set
    by_image_ref[...] = by_image
    weight_copy.wait()
    s1 = jnp.zeros((count, mid), F32)
    s2 = jnp.zeros((count, mid), F32)
    for (first, size), copy in zip(CHUNKS, copies):
        copy.wait()
        part = pl.ds(first, size)
        y = dot32(x_ref[part].reshape(size * count, channels), w_ref[...])
        y = y.reshape(size, count, mid)
        y_ref[part] = y
        s1 += jnp.sum(y, 0)
        s2 += jnp.sum(y * y, 0)
    core = core_ref[0]
    split_halves(core, reorder(by_set, s1), keep_ref, send_ref, 0)
    split_halves(core, reorder(by_set, s2), keep_ref, send_ref, mid // 2)
    next_copy.wait()


def reduce_stage(me, core, x, weight, shuffle, later):
    places, count, channels = x.shape
    mid = weight.shape[1]
    sets = shuffle.shape[1] // count
    hbm = pl.BlockSpec(memory_space=pltpu.HBM)
    return pl.pallas_call(
        reduce_kernel,
        name="reduce",
        in_specs=[SMEM, SMEM, hbm, hbm, hbm, hbm],
        out_specs=[VMEM] * 7,
        out_shape=[
            jax.ShapeDtypeStruct((places, count, mid), F32),
            jax.ShapeDtypeStruct((count, mid), F32),
            jax.ShapeDtypeStruct((count, mid), F32),
            jax.ShapeDtypeStruct((sets, 3 * count), BF16),
            jax.ShapeDtypeStruct((count, 3 * sets), BF16),
            jax.ShapeDtypeStruct(x.shape, x.dtype),
            jax.ShapeDtypeStruct(later.shape, later.dtype),
        ],
        scratch_shapes=[
            pltpu.VMEM(weight.shape, weight.dtype),
            pltpu.VMEM(shuffle.shape, shuffle.dtype),
            pltpu.SemaphoreType.DMA((len(CHUNKS) + 3,)),
        ],
        compiler_params=pltpu.CompilerParams(vmem_limit_bytes=24 * 1024 * 1024),
        cost_estimate=pl.CostEstimate(
            flops=2 * places * count * channels * mid,
            bytes_accessed=2 * x.size + 4 * places * count * mid,
            transcendentals=0,
        ),
    )(
        me,
        core,
        *[pltpu.with_memory_space_constraint(v, pltpu.HBM) for v in (x, weight, shuffle, later)],
    )


def scale_shift(core, mine, other, onehot, gain, shift, rows):
    half = mine.shape[1] // 2
    total1 = join_halves(core, mine[:, :half], other[:, :half])
    total2 = join_halves(core, mine[:, half:], other[:, half:])
    average = total1 / rows
    spread = total2 / rows - average * average
    scale = lax.rsqrt(spread + EPS) * gain
    return reorder(onehot, scale), reorder(onehot, shift - average * scale)


ROW_GROUPS = ((0,), (1, 2), (3, 4, 5), (6,))


def conv_kernel(
    rows,
    core_ref,
    y_ref,
    mine_ref,
    other_ref,
    by_set_ref,
    by_image_ref,
    gain_ref,
    shift_ref,
    w_ref,
    z_ref,
    keep_ref,
    send_ref,
    act,
):
    side = SIDE
    _, count, mid = y_ref.shape
    scale, shift = scale_shift(
        core_ref[0],
        mine_ref[...],
        other_ref[...],
        by_image_ref[...],
        gain_ref[...],
        shift_ref[...],
        rows,
    )
    ready = 0
    s1 = jnp.zeros((count, mid), F32)
    s2 = jnp.zeros((count, mid), F32)
    for group in ROW_GROUPS:
        first, last = group[0], group[-1]
        for row in range(ready, min(side, last + 2)):
            a = y_ref[row * side : (row + 1) * side] * scale[None] + shift[None]
            act[row] = jnp.maximum(a, 0.0).astype(BF16)
        ready = min(side, last + 2)
        dys = [dy for dy in (-1, 0, 1) if first + dy >= 0 and last + dy < side]
        for dx in (0, -1, 1):
            lo, hi = max(0, -dx), side - max(0, dx)
            window = [
                act[first + dy : last + 1 + dy, lo + dx : hi + dx].reshape(-1, mid) for dy in dys
            ]
            weight = [w_ref[3 * (dy + 1) + dx + 1] for dy in dys]
            part = dot32(jnp.concatenate(window, 1), jnp.concatenate(weight, 0))
            part = part.reshape(len(group), hi - lo, count, mid)
            for n, row in enumerate(group):
                if dx == 0:
                    z_ref[row * side : (row + 1) * side] = part[n]
                else:
                    z_ref[row * side + lo : row * side + hi] += part[n]
        z = z_ref[first * side : (last + 1) * side]
        s1 += jnp.sum(z, 0)
        s2 += jnp.sum(z * z, 0)
    core, by_set = core_ref[0], by_set_ref[...]
    split_halves(core, reorder(by_set, s1), keep_ref, send_ref, 0)
    split_halves(core, reorder(by_set, s2), keep_ref, send_ref, mid // 2)


def conv_stage(rows, core, y, mine, other, by_set, by_image, gain, shift, weight):
    places, count, mid = y.shape
    return pl.pallas_call(
        functools.partial(conv_kernel, rows),
        name="conv",
        in_specs=[SMEM] + [VMEM] * 8,
        out_specs=[VMEM] * 3,
        out_shape=[
            jax.ShapeDtypeStruct((places, count, mid), F32),
            jax.ShapeDtypeStruct((count, mid), F32),
            jax.ShapeDtypeStruct((count, mid), F32),
        ],
        scratch_shapes=[pltpu.VMEM((SIDE, SIDE, count, mid), BF16)],
        compiler_params=pltpu.CompilerParams(vmem_limit_bytes=16 * 1024 * 1024),
        cost_estimate=pl.CostEstimate(
            flops=2 * 361 * count * mid * mid,
            bytes_accessed=8 * places * count * mid + 2 * weight.size,
            transcendentals=0,
        ),
    )(core, y, mine, other, by_set, by_image, gain, shift, weight)


COLUMNS = 256


def center_kernel(gain_ref, shift_ref, w_ref, act_center_ref, center_ref):
    gain, shift = gain_ref[...], shift_ref[...]
    ratio = jnp.abs(shift) / gain
    value = jnp.maximum(shift, 0.0) + 0.4 * gain * jnp.exp(-ratio * (1.1 + 0.45 * ratio))
    value = value.astype(BF16)
    act_center_ref[...] = value.astype(F32)
    wide = dot32(jnp.broadcast_to(value, (16, value.shape[1])), w_ref[...])
    center_ref[...] = wide[:1]


def center_stage(gain, shift, weight):
    return pl.pallas_call(
        center_kernel,
        name="center",
        in_specs=[VMEM] * 3,
        out_specs=[VMEM] * 2,
        out_shape=[
            jax.ShapeDtypeStruct(gain.shape, F32),
            jax.ShapeDtypeStruct((1, weight.shape[1]), F32),
        ],
        compiler_params=pltpu.CompilerParams(vmem_limit_bytes=8 * 1024 * 1024),
        cost_estimate=pl.CostEstimate(
            flops=32 * weight.size, bytes_accessed=2 * weight.size, transcendentals=gain.size
        ),
    )(gain, shift, weight)


def expand_kernel(
    rows,
    core_ref,
    z_ref,
    mine_ref,
    other_ref,
    by_set_ref,
    by_image_ref,
    gain_ref,
    shift_ref,
    act_center_ref,
    center_ref,
    w_ref,
    e_ref,
    keep_ref,
    send_ref,
    act,
    sq_s,
):
    places, count, mid = z_ref.shape
    wide = w_ref.shape[1]
    core = core_ref[0]
    by_set = by_set_ref[...]
    scale, shift = scale_shift(
        core,
        mine_ref[...],
        other_ref[...],
        by_image_ref[...],
        gain_ref[...],
        shift_ref[...],
        rows,
    )
    total = jnp.zeros((count, mid), F32)
    for row in range(0, places, SIDE):
        a = z_ref[row : row + SIDE] * scale[None] + shift[None]
        a = jnp.maximum(a, 0.0).astype(BF16)
        act[row : row + SIDE] = a
        total += jnp.sum(a.astype(F32), 0)
    flat = act[...].reshape(places * count, mid)
    for j in range(0, wide, COLUMNS):
        e = dot32(flat, w_ref[:, j : j + COLUMNS]).reshape(places, count, COLUMNS)
        e_ref[:, :, j : j + COLUMNS] = e
        d = e - center_ref[:, j : j + COLUMNS][None]
        sq_s[:, j : j + COLUMNS] = jnp.sum(d * d, 0)
    total = total - places * act_center_ref[...]
    split_halves(core, reorder(by_set, total), keep_ref, send_ref, 0)
    split_halves(core, reorder(by_set, sq_s[...]), keep_ref, send_ref, mid // 2)


def expand_stage(
    rows, core, z, mine, other, by_set, by_image, gain, shift, act_center, center, weight
):
    places, count, mid = z.shape
    wide = weight.shape[1]
    sums = (mid + wide) // 2
    return pl.pallas_call(
        functools.partial(expand_kernel, rows),
        name="expand",
        in_specs=[SMEM] + [VMEM] * 10,
        out_specs=[VMEM] * 3,
        out_shape=[
            jax.ShapeDtypeStruct((places, count, wide), F32),
            jax.ShapeDtypeStruct((count, sums), F32),
            jax.ShapeDtypeStruct((count, sums), F32),
        ],
        scratch_shapes=[
            pltpu.VMEM((places, count, mid), BF16),
            pltpu.VMEM((count, wide), F32),
        ],
        compiler_params=pltpu.CompilerParams(vmem_limit_bytes=16 * 1024 * 1024),
        cost_estimate=pl.CostEstimate(
            flops=2 * places * count * mid * wide,
            bytes_accessed=4 * places * count * (mid + wide),
            transcendentals=0,
        ),
    )(core, z, mine, other, by_set, by_image, gain, shift, act_center, center, weight)


def merge_kernel(
    rows,
    core_ref,
    e_ref,
    x_ref,
    mine_ref,
    other_ref,
    by_image_ref,
    gain_ref,
    shift_ref,
    act_center_ref,
    center_ref,
    w_ref,
    proj_ref,
    key_ref,
    copies_ref,
    scale_s,
    shift_s,
    pool,
):
    places, count, wide = e_ref.shape
    core, by_image = core_ref[0], by_image_ref[...]
    mine, other = mine_ref[...], other_ref[...]
    cut = w_ref.shape[0] // 2
    sums = join_halves(core, mine[:, :cut], other[:, :cut]) + rows * act_center_ref[...]
    squares = join_halves(core, mine[:, cut:], other[:, cut:])
    three = dot32(pieces(sums), w_ref[...])
    sets = sums.shape[0]
    average = (three[:sets] + (three[sets : 2 * sets] + three[2 * sets :])) / rows
    away = average - center_ref[...]
    spread = squares / rows - away * away
    scale = lax.rsqrt(spread + EPS) * gain_ref[...]
    scale_s[...] = reorder(by_image, scale)
    shift_s[...] = reorder(by_image, shift_ref[...] - average * scale)
    for j in range(0, wide, COLUMNS):
        cols = slice(j, j + COLUMNS)
        sc, sh = scale_s[:, cols], shift_s[:, cols]
        total = jnp.zeros((count, COLUMNS), F32)
        for place in range(places):
            y = e_ref[place, :, cols] * sc + sh + x_ref[place, :, cols].astype(F32)
            total += jnp.maximum(y, 0.0)
        pool[:, cols] = total
    pooled = (pool[...] / places).astype(BF16)
    u = dot32(pooled, proj_ref[...])
    key = (u * lax.rsqrt(jnp.sum(u * u, 1, keepdims=True) + UNIT_EPS)).astype(BF16)
    key_ref[...] = key
    copies_ref[...] = jnp.broadcast_to(key[None], copies_ref.shape)


def merge_stage(
    rows, core, peers, e, x, mine, other, by_image, gain, shift, act_center, center, weight, proj
):
    places, count, wide = e.shape
    feat = proj.shape[1]
    return pl.pallas_call(
        functools.partial(merge_kernel, rows),
        name="merge",
        in_specs=[SMEM] + [VMEM] * 11,
        out_specs=[VMEM] * 2,
        out_shape=[
            jax.ShapeDtypeStruct((count, feat), BF16),
            jax.ShapeDtypeStruct((peers, count, feat), BF16),
        ],
        scratch_shapes=[
            pltpu.VMEM((count, wide), F32),
            pltpu.VMEM((count, wide), F32),
            pltpu.VMEM((count, wide), F32),
        ],
        compiler_params=pltpu.CompilerParams(vmem_limit_bytes=16 * 1024 * 1024),
        cost_estimate=pl.CostEstimate(
            flops=8 * places * count * wide,
            bytes_accessed=2 * x.size + 4 * e.size,
            transcendentals=0,
        ),
    )(core, e, x, mine, other, by_image, gain, shift, act_center, center, weight, proj)


def negative_kernel(factor, q_ref, k_ref, out_ref):
    @pl.when(pl.program_id(0) == 0)
    def _():
        out_ref[...] = jnp.zeros_like(out_ref)

    keys = k_ref[...]
    wide = keys.astype(F32)
    norm = lax.rsqrt(jnp.sum(wide * wide, 1, keepdims=True) + UNIT_EPS) * factor
    score = lax.dot_general(
        keys, q_ref[...], (((1,), (1,)), ((), ())), preferred_element_type=F32
    )
    out_ref[...] += jnp.sum(jnp.exp2(score * norm), 0, keepdims=True)


def negative_stage(queries, keys, part, parts):
    count, feat = queries.shape
    total = keys.shape[0] // parts
    block = math.gcd(total, 2048)
    steps = total // block
    return pl.pallas_call(
        functools.partial(negative_kernel, math.log2(math.e) / TEMP),
        name="negative",
        grid=(steps,),
        in_specs=[VMEM, pl.BlockSpec((block, feat), lambda i: (i + part * steps, 0))],
        out_specs=pl.BlockSpec((1, count), lambda i: (0, 0)),
        out_shape=jax.ShapeDtypeStruct((1, count), F32),
        compiler_params=params(8),
        cost_estimate=pl.CostEstimate(
            flops=2 * total * count * feat,
            bytes_accessed=2 * total * feat,
            transcendentals=total * count,
        ),
    )(queries, keys)


def loss_kernel(table_ref, u_ref, pos_ref, neg_ref, loss_ref):
    logits = lax.dot_general(
        table_ref[...], u_ref[...], (((1,), (1,)), ((), ())), preferred_element_type=F32
    )
    row = lax.broadcasted_iota(jnp.int32, logits.shape, 0)
    picked = jnp.sum(jnp.where(row == pos_ref[...], logits, 0.0), 0, keepdims=True) / TEMP
    loss_ref[...] = jnp.log(jnp.exp(picked) + neg_ref[...]) - picked


def loss_stage(table, units, positive, negatives):
    return pl.pallas_call(
        loss_kernel,
        name="loss",
        in_specs=[VMEM] * 4,
        out_specs=VMEM,
        out_shape=jax.ShapeDtypeStruct(positive.shape, F32),
        compiler_params=pltpu.CompilerParams(vmem_limit_bytes=8 * 1024 * 1024),
    )(table, units, positive, negatives)


def unit_rows(values):
    as_float = values.astype(F32)
    return (
        as_float * lax.rsqrt(jnp.sum(as_float * as_float, -1, keepdims=True) + UNIT_EPS)
    ).astype(BF16)


RING = 4


def swap_core():
    return [(i, i ^ 1) for i in range(2 * RING * RING)]


def mixed(v):
    return (v >> 1) & 1


def ring_swap(k, flip):
    pairs = []
    for i in range(2 * RING * RING):
        x, z, c = i // (2 * RING), (i // 2) % RING, i % 2
        half = c ^ mixed(x) ^ mixed(z)
        if (half == 1) != flip:
            x = x ^ k
        else:
            z = z ^ k
        pairs.append((i, (x * RING + z) * 2 + (half ^ mixed(x) ^ mixed(z))))
    return pairs


def queue_swap(values, k):
    return lax.ppermute(values, "queue", [(i, i ^ k) for i in range(RING)])


def reduce_sets(keep, send, side_work, side_input, wire):
    total = keep + lax.ppermute(send, "dp", swap_core())
    for turn, work in enumerate(side_work):
        parts = []
        sent = total.astype(wire)
        for k in (1, 2, 3):
            parts.append(lax.ppermute(sent, "dp", ring_swap(k, turn == 1)).astype(F32))
        held, free = work(lax.optimization_barrier((side_input, total))[0])
        parts, held = lax.optimization_barrier((parts, held))
        side_input = (held, free)
        total = (total + parts[0]) + (parts[1] + parts[2])
    return total, lax.ppermute(total, "dp", swap_core()), side_input


def on_device(
    features,
    shuffle,
    positive,
    queries,
    queue_keys,
    reduce_weight,
    gain_one,
    shift_one,
    w_spatial,
    gain_two,
    shift_two,
    w_expand,
    gain_three,
    shift_three,
    w_project,
):
    count, places, _ = features.shape
    peers = lax.axis_size("dp")
    me = lax.axis_index("dp").astype(jnp.int32)
    core = me ^ mixed(me >> 3) ^ mixed((me >> 1) & 3)
    core = jnp.bitwise_and(core, 1).reshape(1)
    rows = count * places
    x = jnp.transpose(features, (1, 0, 2))
    gain_two, shift_two = gain_two[None], shift_two[None]

    def negative_one(state):
        here, gain, shift = state
        here = unit_rows(here)
        centers = center_stage(gain, shift, w_expand)
        return (here, negative_stage(here, queue_keys, 0, 2), centers), None

    def negative_two(state):
        here, sums, centers = state[0]
        return (here, sums + negative_stage(here, queue_keys, 1, 2), centers), None

    def nothing(state):
        return None, None

    first = queue_swap(queries, 1)
    y, keep, send, by_set, by_image, x, w_spatial = reduce_stage(
        me.reshape(1), core, x, reduce_weight, shuffle, w_spatial
    )
    pair = jnp.concatenate([queries, first], 0)
    mine, other, _ = reduce_sets(keep, send, (nothing, nothing), None, F32)
    asked = jnp.concatenate([pair, queue_swap(pair, 3)], 0)
    z, keep, send = conv_stage(
        rows, core, y, mine, other, by_set, by_image, gain_one[None], shift_one[None], w_spatial
    )
    mine, other, ((units, sums, centers), _) = reduce_sets(
        keep, send, (negative_one, negative_two), (asked, gain_two, shift_two), F32
    )
    told = queue_swap(sums[:, 2 * count :], 3)
    e, keep, send = expand_stage(
        rows, core, z, mine, other, by_set, by_image, gain_two, shift_two, *centers, w_expand
    )
    mine, other, _ = reduce_sets(keep, send, (nothing, nothing), None, BF16)
    sums = sums[:, : 2 * count] + told
    told = queue_swap(sums[:, count:], 1)
    key_rows, copies = merge_stage(
        rows,
        core,
        peers,
        e,
        x,
        mine,
        other,
        by_image,
        gain_three[None],
        shift_three[None],
        *centers,
        w_expand,
        w_project,
    )
    table = lax.all_to_all(copies, "dp", split_axis=0, concat_axis=0, tiled=True)
    table = table.reshape(peers * count, -1)
    negatives = sums[:, :count] + told
    loss_vals = loss_stage(table, units[:count], positive.reshape(1, count), negatives)
    return (loss_vals.reshape(count), key_rows)


def solution(mesh):
    placed = (
        P(("queue", "dp"), None, None),
        P("queue", None),
        P(("queue", "dp")),
        P(("queue", "dp"), None),
        P("queue", None),
    ) + (P(),) * 10
    return jax.shard_map(
        on_device,
        mesh=mesh,
        in_specs=placed,
        out_specs=(P(("queue", "dp")), P(("queue", "dp"), None)),
        check_vma=False,
    )
```
